32 devices in a mesh: gx: 8 (over y, x, core), gy: 4 (over z).
Axes of the slice: x: 2, y: 2, z: 4, core: 2. Of those that a mesh axis runs over, the one named last changes fastest.
Arguments:
- dual_ops: float32 [8, 4, 1536, 1536], P('gx', 'gy')
- loads: float32 [8, 4, 2, 384, 128], P('gx', 'gy'), may hold values from -16 to 16
- coarse_rhs: float32 [8, 4, 6, 128], P('gx', 'gy'), may hold values from -288 to 288
- coarse_modes: float32 [8, 4, 2, 2, 6, 384], P('gx', 'gy'), as said below
- free_mask: int32 [8, 4, 2, 384], P('gx', 'gy'), may hold values from 0 to 1
- face_match: int32 [8, 4, 2, 384], P('gx', 'gy'), may hold values from 0 to 383, each once within a row
- coarse_rows: float32 [8, 4, 3, 6, 192], P('gx', 'gy'), as said below
Outputs:
- multipliers: float32 [8, 4, 2, 384, 128], P('gx', 'gy')
- projected: float32 [8, 4, 2, 384, 128], P('gx', 'gy')
The draws below stay inside these ranges and needn't reach their ends.
Inputs may be any that keep to these rules, and one draw needn't show every extreme that they name: The draws of coarse_modes, free_mask and coarse_rows belong together. coarse_modes[a,b,0,1] is zero on the last grid column and coarse_modes[a,b,1,1] on the last grid row. With C the symmetric positive definite coarse matrix whose entries are the sums of free times products of the coarse-mode images of two modes over all east and south face multipliers (G^T G restricted to free multipliers, in the order (a, b, mode)), coarse_rows[a,b,0] are the rows of the inverse of C for the modes of (a,b), up to rounding; coarse_rows[a,b,1] equals coarse_rows[a,b+1,0] and coarse_rows[a,b,2] equals coarse_rows[a+1,b,0], zero where that neighbour does not exist.
All inputs are finite; a program needn't handle non-finite values.
Results may differ from the reference program's by a relative error of at most 0.00029.
Values sent between devices are 32-bit elements; how exact they have to be, the bound alone decides.
A program may use at most 64 MiB of HBM per device.

```python
import jax
import jax.numpy as jnp
from jax import lax

LM = 1536
LF = 384
ITERS = 3
NCASE = 128
SX = 8
SY = 4
NC = 192


def coarse_frame(key):
    base = jax.random.fold_in(key, 9173)
    key_dirs, key_plane, key_weight, key_mask, key_other = jax.random.split(base, 5)
    directions = jax.random.normal(key_dirs, (SX, SY, 2, LF, 3), jnp.float32)
    directions = directions / jnp.sqrt(jnp.sum(directions * directions, axis=-1, keepdims=True) + 1e-06)
    plane = jax.random.uniform(key_plane, (SX, SY, 2, LF, 2), jnp.float32, -0.5, 0.5)
    face_index = jnp.arange(2)[None, None, :, None]
    first = jnp.where(face_index == 0, 0.5, plane[..., 0])
    second = jnp.where(face_index == 0, plane[..., 0], 0.5)
    points = jnp.stack([first, second, plane[..., 1]], axis=-1)
    weights = jnp.exp(jax.random.uniform(key_weight, (SX, SY, 2, LF), jnp.float32, jnp.log(0.5), jnp.log(2.0)))
    other_weights = jnp.exp(jax.random.uniform(key_other, (SX, SY, 2, LF), jnp.float32, jnp.log(0.5), jnp.log(2.0)))

    def images_at(where, scale):
        rotation = jnp.cross(where, directions)
        return jnp.concatenate([directions, rotation], axis=-1) * scale[..., None]
    offsets = jnp.array([[1.0, 0.0, 0.0], [0.0, 1.0, 0.0]], jnp.float32)[None, None, :, None, :]
    own_images = images_at(points, weights)
    other_images = -images_at(points - offsets, other_weights)
    row_index = jnp.arange(SX)[:, None, None, None]
    col_index = jnp.arange(SY)[None, :, None, None]
    exists = jnp.where(face_index == 0, col_index < SY - 1, row_index < SX - 1)
    other_images = other_images * exists[..., None].astype(jnp.float32)
    modes = jnp.stack([own_images, other_images], axis=3)
    modes = jnp.transpose(modes, (0, 1, 2, 3, 5, 4))
    mask = (jax.random.randint(key_mask, (SX, SY, 2, LF), 0, 8) < 6).astype(jnp.int32)
    empty = jnp.zeros((SX, SY, 6, LF), jnp.float32)
    own_part = jnp.stack([modes[:, :, 0, 0], modes[:, :, 1, 0]], axis=3)
    east_part = jnp.stack([modes[:, :, 0, 1], empty], axis=3)
    south_part = jnp.stack([empty, modes[:, :, 1, 1]], axis=3)
    kernel = jnp.stack([own_part, east_part, south_part], axis=2)
    masked = kernel * mask[:, :, None, None, :, :].astype(jnp.float32)
    blocks = jnp.einsum('abrjfk,absifk->abrjsi', masked, kernel, precision=lax.Precision.HIGHEST)
    row_moves = [jnp.eye(SX, SX, 0), jnp.eye(SX, SX, 0), jnp.eye(SX, SX, 1)]
    col_moves = [jnp.eye(SY, SY, 0), jnp.eye(SY, SY, 1), jnp.eye(SY, SY, 0)]
    coarse = jnp.zeros((SX, SY, 6, SX, SY, 6), jnp.float32)
    for first_role in range(3):
        for second_role in range(3):
            coarse = coarse + jnp.einsum('abji,ac,bd,ae,bf->cdjefi', blocks[:, :, first_role, :, second_role, :], row_moves[first_role], col_moves[first_role], row_moves[second_role], col_moves[second_role], precision=lax.Precision.HIGHEST)
    coarse = coarse.reshape(NC, NC)
    inverse = jnp.linalg.inv(coarse)
    identity = jnp.eye(NC, dtype=jnp.float32)
    inverse = jnp.dot(inverse, 2.0 * identity - jnp.dot(coarse, inverse, precision=lax.Precision.HIGHEST), precision=lax.Precision.HIGHEST)
    inverse = 0.5 * (inverse + inverse.T)
    grid_rows = inverse.reshape(SX, SY, 6, NC)
    padded = jnp.pad(grid_rows, ((0, 1), (0, 1), (0, 0), (0, 0)))
    rows = jnp.stack([grid_rows, padded[:SX, 1:SY + 1], padded[1:SX + 1, :SY]], axis=2)
    return (modes, mask, rows)


def draw_coarse_modes(key, part):
    return coarse_frame(key)[0]


def draw_free_mask(key, part):
    return coarse_frame(key)[1]


def draw_coarse_rows(key, part):
    return coarse_frame(key)[2]


def draw_dual_ops(key, part):
    base = jax.random.fold_in(key, 31)
    key_noise, key_diag, key_scale = jax.random.split(base, 3)
    noise = jax.random.normal(key_noise, (SX, SY, LM, LM), jnp.float32)
    noise = (noise + jnp.swapaxes(noise, 2, 3)) / jnp.sqrt(2.0 * LM)
    diagonal = jax.random.uniform(key_diag, (SX, SY, LM), jnp.float32, 2.5, 4.0)
    scales = jnp.exp(jax.random.uniform(key_scale, (SX, SY, LM), jnp.float32, jnp.log(0.5), jnp.log(2.0)))
    matrix = noise + diagonal[..., None] * jnp.eye(LM, dtype=jnp.float32)
    return scales[..., :, None] * scales[..., None, :] * matrix


def draw_loads(key, part):
    base = jax.random.fold_in(key, 57)
    position = (jnp.arange(SX)[:, None] * SY + jnp.arange(SY)[None, :]).astype(jnp.float32) / (SX * SY - 1)
    values = jax.random.truncated_normal(base, -4.0, 4.0, (SX, SY, 2, LF, NCASE), jnp.float32)
    ramp = jnp.power(3.0, position)
    return values * ramp[:, :, None, None, None]


def level_of(stream_key, dims, pieces, least, largest):
    def one(dim, parts):
        steps = jax.random.uniform(jax.random.fold_in(jax.random.fold_in(stream_key, 6), dim), (parts,), jnp.float32, least / len(pieces), largest / len(pieces))
        return jnp.repeat(jnp.exp(steps), dims[dim] // parts).reshape((-1,) + (1,) * (len(dims) - dim - 1))

    factor_of = one(*pieces[0])
    for cut in pieces[1:]:
        factor_of = factor_of * one(*cut)
    return factor_of


def scatter_about(own_key, dims, deviation, bound, cuts=(), kind=jnp.bfloat16):
    drawn = jax.random.normal(own_key, dims, jnp.float32) * deviation
    if len(cuts) > 0:
        drawn = level_of(own_key, dims, cuts, -0.22, 0.18) * drawn
    return jnp.clip(drawn, min=-bound, max=bound).astype(kind)


def setup_inputs(seed: int = 0) -> dict:
    arg_keys = jax.random.split(jax.random.key(seed), 8)
    dual_ops = draw_dual_ops(jax.random.fold_in(arg_keys[7], 71), 0)
    loads = draw_loads(jax.random.fold_in(arg_keys[7], 71), 0)
    coarse_rhs = scatter_about(arg_keys[2], (SX, SY, 6, NCASE), (LF // 8), 288.0, ((0, 8), (1, 4)), jnp.float32)
    coarse_modes = draw_coarse_modes(jax.random.fold_in(arg_keys[7], 71), 0)
    free_mask = draw_free_mask(jax.random.fold_in(arg_keys[7], 71), 0)
    face_match = jax.vmap(lambda own: jax.random.permutation(own, LF))(jax.random.split(arg_keys[5], SX * SY * 2)).reshape((SX, SY, 2, LF)).astype(jnp.int32)
    coarse_rows = draw_coarse_rows(jax.random.fold_in(arg_keys[7], 71), 0)
    return dict(dual_ops=dual_ops, loads=loads, coarse_rhs=coarse_rhs, coarse_modes=coarse_modes, free_mask=free_mask, face_match=face_match, coarse_rows=coarse_rows)


HIGHEST = lax.Precision.HIGHEST

def lower_shift(values, dimension):
    widths = [(0, 0)] * values.ndim
    widths[dimension] = (1, 0)
    return lax.slice_in_dim(jnp.pad(values, widths), 0, values.shape[dimension], axis=dimension)

def upper_shift(values, dimension):
    widths = [(0, 0)] * values.ndim
    widths[dimension] = (0, 1)
    return lax.slice_in_dim(jnp.pad(values, widths), 1, values.shape[dimension] + 1, axis=dimension)

def pick_rows(values, indices):
    full_index = jnp.broadcast_to(indices[..., None], values.shape)
    return jnp.take_along_axis(values, full_index, axis=2)

def apply_dual(dual_ops, face_match, free_slots, field):
    face_slots = field.shape[3]
    case_count = field.shape[4]
    from_west = lower_shift(field[:, :, 0], 1)
    from_north = lower_shift(field[:, :, 1], 0)
    west_side = -pick_rows(from_west, face_match[:, :, 0])
    north_side = -pick_rows(from_north, face_match[:, :, 1])
    stacked = jnp.concatenate([field[:, :, 0], field[:, :, 1], west_side, north_side], axis=2)
    product = jnp.einsum('abij,abjc->abic', dual_ops, stacked, precision=HIGHEST)
    product = product.reshape(product.shape[0], product.shape[1], 4, face_slots, case_count)
    inverse = jnp.argsort(face_match, axis=-1).astype(jnp.int32)
    back_west = upper_shift(pick_rows(product[:, :, 2], inverse[:, :, 0]), 1)
    back_north = upper_shift(pick_rows(product[:, :, 3], inverse[:, :, 1]), 0)
    return (product[:, :, :2] - jnp.stack([back_west, back_north], axis=2)) * free_slots

def coarse_terms(coarse_modes, field):
    own_terms = jnp.einsum('abfjk,abfkc->abjc', coarse_modes[:, :, :, 0], field, precision=HIGHEST)
    east_terms = jnp.einsum('abjk,abkc->abjc', coarse_modes[:, :, 0, 1], field[:, :, 0], precision=HIGHEST)
    south_terms = jnp.einsum('abjk,abkc->abjc', coarse_modes[:, :, 1, 1], field[:, :, 1], precision=HIGHEST)
    return (own_terms, east_terms, south_terms)

def coarse_solve(coarse_rows, own_terms, east_terms, south_terms):
    summed = own_terms + lower_shift(east_terms, 1) + lower_shift(south_terms, 0)
    flat = summed.reshape(-1, summed.shape[-1])
    return jnp.einsum('abrjn,nc->abrjc', coarse_rows, flat, precision=HIGHEST)

def mode_images(coarse_modes, free_slots, alpha):
    east_face = jnp.einsum('abjk,abjc->abkc', coarse_modes[:, :, 0, 0], alpha[:, :, 0], precision=HIGHEST)
    east_face = east_face + jnp.einsum('abjk,abjc->abkc', coarse_modes[:, :, 0, 1], alpha[:, :, 1], precision=HIGHEST)
    south_face = jnp.einsum('abjk,abjc->abkc', coarse_modes[:, :, 1, 0], alpha[:, :, 0], precision=HIGHEST)
    south_face = south_face + jnp.einsum('abjk,abjc->abkc', coarse_modes[:, :, 1, 1], alpha[:, :, 2], precision=HIGHEST)
    return jnp.stack([east_face, south_face], axis=2) * free_slots

def reference(dual_ops, loads, coarse_rhs, coarse_modes, free_mask, face_match, coarse_rows):
    free_slots = free_mask.astype(jnp.float32)[..., None]

    def project(field):
        own_terms, east_terms, south_terms = coarse_terms(coarse_modes, field)
        alpha = coarse_solve(coarse_rows, own_terms, east_terms, south_terms)
        return field - mode_images(coarse_modes, free_slots, alpha)
    zeros_rhs = jnp.zeros_like(coarse_rhs)
    multipliers = mode_images(coarse_modes, free_slots, coarse_solve(coarse_rows, coarse_rhs, zeros_rhs, zeros_rhs))
    gradient = apply_dual(dual_ops, face_match, free_slots, multipliers) - loads * free_slots
    projected = project(gradient)
    norm_now = jnp.sum(projected * projected, axis=(0, 1, 2, 3))
    direction = projected
    for step in range(ITERS):
        image = apply_dual(dual_ops, face_match, free_slots, direction)
        step_size = norm_now / jnp.sum(direction * image, axis=(0, 1, 2, 3))
        multipliers = multipliers + step_size * direction
        gradient = gradient + step_size * image
        projected = project(gradient)
        norm_next = jnp.sum(projected * projected, axis=(0, 1, 2, 3))
        if step + 1 < ITERS:
            direction = projected + norm_next / norm_now * direction
            norm_now = norm_next
    return (multipliers, projected)
```

```python
import functools

import jax
import jax.numpy as jnp
from jax import lax
from jax.experimental import pallas as pl
from jax.experimental.pallas import tpu as pltpu
from jax.sharding import PartitionSpec as P

ITERS = 3
F32 = jnp.float32
BF16 = jnp.bfloat16
MESH = pl.DeviceIdType.MESH
EAST, SOUTH, WEST, NORTH = 0, 1, 2, 3
OPPOSITE = (WEST, NORTH, EAST, SOUTH)
ROUNDS = ITERS + 2
APPLIES = ITERS + 1


def split(values):
    high = values.astype(BF16)
    low = (values - high.astype(F32)).astype(BF16)
    return high, low


def dot32(left, right):
    return jnp.dot(left, right, preferred_element_type=F32)


def kernel(
    nx, ny, a_hbm, loads_hbm, rhs_ref, modes_ref, free_ref, match_ref, rows_ref,
    mult_ref, proj_ref,
    a_stage, a_high, a_low, loads4, pack, nb_pack, inverse, terms, alphas, alpha_pair,
    gt8, g_high, g_low, fg_high, fg_low, free4, put, perm, perm_back, vsplit, u_split,
    outbox, inbox, p_f, d_f, q_f, fp_f, fq_f,
    a_sem, l_sem, face_send, face_recv, pk_send, pk_recv, ld_send, ld_recv,
    gy_send, gy_recv, gx_send, gx_recv, cy_send, cy_recv, cx_send, cx_recv, t_send, t_recv,
):
    lf = free_ref.shape[1]
    nc = mult_ref.shape[1]
    lm = a_high.shape[0]
    ncoarse = rows_ref.shape[2]
    others = nx * ny - 1
    wide = inverse.shape[3]
    me_x = lax.axis_index("gx")
    me_y = lax.axis_index("gy")
    exists = (me_y < ny - 1, me_x < nx - 1, me_y > 0, me_x > 0)
    place = ((me_x, me_y + 1), (me_x + 1, me_y), (me_x, me_y - 1), (me_x - 1, me_y))

    def face(f):
        return pl.ds(f * lf, lf)

    chunk = lm // 6
    a_copies = [
        pltpu.make_async_copy(
            a_hbm.at[pl.ds(i * chunk, chunk)], a_stage.at[pl.ds(i * chunk, chunk)], a_sem.at[i]
        )
        for i in range(6)
    ]
    for copy in a_copies:
        copy.start()
    l_copy = pltpu.make_async_copy(loads_hbm, loads4.at[pl.ds(0, 2 * lf)], l_sem)
    l_copy.start()

    barrier = pltpu.get_barrier_semaphore()
    for t in range(1, nx):
        pl.semaphore_signal(
            barrier, inc=1, device_id=(lax.rem(me_x + t, nx), me_y), device_id_type=MESH
        )
    for t in range(1, ny):
        pl.semaphore_signal(
            barrier, inc=1, device_id=(me_x, lax.rem(me_y + t, ny)), device_id_type=MESH
        )

    pack[...] = jnp.zeros_like(pack)
    for f in range(2):
        pack[f, 0:6, :] = modes_ref[f, :, 0, :]
        pack[f, 8:14, :] = modes_ref[f, :, 1, :]
        pack[f, 16:17, :] = free_ref[f : f + 1, :].astype(F32)

    row = lax.broadcasted_iota(jnp.int32, (ncoarse, wide), 0)
    col = lax.broadcasted_iota(jnp.int32, (ncoarse, wide), 1)
    slot = jnp.bitwise_and(col, 7)
    spread = jnp.where((row == 6 * jnp.right_shift(col, 3) + slot) & (slot < 6), 1.0, 0.0)
    inverse[me_x, me_y] = jnp.zeros((8, wide), F32)
    inverse[me_x, me_y, 0:6, :] = jnp.dot(
        rows_ref[0:6, 0, :], spread.astype(F32), precision=lax.Precision.HIGHEST,
        preferred_element_type=F32,
    )
    terms[0, me_x, me_y] = jnp.zeros((16, nc), F32)
    terms[0, me_x, me_y, 0:6, :] = rhs_ref[:, 0, :]

    pl.semaphore_wait(barrier, nx + ny - 2)

    def remote(src, dst, send, recv, where):
        return pltpu.make_async_remote_copy(
            src_ref=src, dst_ref=dst, send_sem=send, recv_sem=recv,
            device_id=where, device_id_type=MESH,
        )

    def neighbour_copy(f, src, dst, send, recv):
        return remote(src, dst, send, recv, place[f])

    for f in range(2):
        @pl.when(exists[f])
        def _():
            neighbour_copy(f, pack.at[f], nb_pack.at[f], pk_send.at[f], pk_recv.at[f]).start()

    def spread_column(view, send, recv):
        copies = []
        for t in range(1, ny):
            copies.append(remote(
                view(me_x, me_y), view(me_x, me_y), send.at[t], recv.at[t],
                (me_x, lax.rem(me_y + t, ny)),
            ))
        return copies

    def spread_row(view, send, recv):
        copies = []
        for t in range(1, nx):
            copies.append(remote(
                view(me_x), view(me_x), send.at[t], recv.at[t],
                (lax.rem(me_x + t, nx), me_y),
            ))
        return copies

    pending = []

    def begin(copies):
        for copy in copies:
            copy.start()
        pending.extend(copies)

    def finish(copies):
        for copy in copies:
            copy.wait_recv()

    def terms_column(r, rows):
        return spread_column(
            lambda x, y: terms.at[r, x, y, pl.ds(0, rows)], gy_send, gy_recv
        )

    def terms_row(r, rows):
        return spread_row(
            lambda x: terms.at[r, x, :, pl.ds(0, rows)], gx_send, gx_recv
        )

    inv_col = spread_column(lambda x, y: inverse.at[x, y], cy_send, cy_recv)
    inv_row = spread_row(lambda x: inverse.at[x], cx_send, cx_recv)
    rhs_col = terms_column(0, 8)
    rhs_row = terms_row(0, 8)
    begin(rhs_col)
    begin(inv_col)
    for f in range(2):
        @pl.when(exists[f])
        def _():
            neighbour_copy(
                f, loads_hbm.at[face(f)], loads4.at[face(2 + f)], ld_send.at[f], ld_recv.at[f]
            ).start()

    for f in range(4):
        @pl.when(jnp.logical_not(exists[f]))
        def _():
            for r in range(APPLIES):
                inbox[r, f] = jnp.zeros((lf, nc), F32)
    for f in range(2):
        @pl.when(jnp.logical_not(exists[2 + f]))
        def _():
            nb_pack[f] = jnp.zeros((24, lf), F32)
            loads4[face(2 + f), :] = jnp.zeros((lf, nc), F32)

    slots = lax.broadcasted_iota(jnp.int32, (lf, lf), 0)
    for f in range(2):
        back = jnp.where(slots == match_ref[f : f + 1, :], 1.0, 0.0).astype(F32)
        perm_back[f] = back.astype(BF16)
        perm[f] = (-jnp.transpose(back)).astype(BF16)

    def cast_chunk(i):
        a_copies[i].wait()
        part = a_stage[pl.ds(i * chunk, chunk), :]
        high, low = split(part)
        a_high[pl.ds(i * chunk, chunk), :] = high
        a_low[pl.ds(i * chunk, chunk), :] = low

    for i in range(3):
        cast_chunk(i)

    finish(rhs_col)
    begin(rhs_row)
    finish(inv_col)
    begin(inv_row)

    for i in range(3, 6):
        cast_chunk(i)

    for f in range(2):
        @pl.when(exists[2 + f])
        def _():
            neighbour_copy(f, pack.at[f], nb_pack.at[f], pk_send.at[f], pk_recv.at[f]).wait_recv()

    for f in range(4):
        put[...] = jnp.zeros_like(put)
        source = pack if f < 2 else nb_pack
        mask = source[f % 2, 16:17, :]
        owner = source[f % 2, 0:8, :] * mask
        other = source[f % 2, 8:16, :] * mask
        own_part, far_part = (owner, other) if f < 2 else (other, owner)
        put[0:8, :] = own_part
        put[8 * (f + 1) : 8 * (f + 2), :] = far_part
        high, low = split(own_part)
        gt8[0:8, face(f)] = high.astype(F32)
        gt8[8:16, face(f)] = low.astype(F32)
        q_f[face(f), :] = jnp.transpose(put[...])
        free4[face(f), :] = jnp.transpose(jnp.broadcast_to(mask, (nc, lf)))
    high, low = split(q_f[...])
    g_high[...] = high
    g_low[...] = low

    def split_field(ref):
        high, low = split(ref[...])
        vsplit[:, 0:nc] = high
        vsplit[:, nc : 2 * nc] = low

    def coarse_terms(r):
        both = dot32(gt8[...].astype(BF16), vsplit[...])
        terms[r, me_x, me_y, 0:8, :] = (
            both[0:8, 0:nc] + both[0:8, nc : 2 * nc] + both[8:16, 0:nc]
        )
        terms[r, me_x, me_y, 8:16, :] = jnp.zeros((8, nc), F32)

    def face_copy(r, f):
        g = OPPOSITE[f]
        return neighbour_copy(
            f, outbox.at[r, f], inbox.at[r, g], face_send.at[r, f], face_recv.at[r, g]
        )

    def apply_start(r, between):
        u_split[face(EAST), :] = vsplit[face(EAST), :]
        u_split[face(SOUTH), :] = vsplit[face(SOUTH), :]
        for f in range(2):
            u_split[face(2 + f), :] = dot32(perm[f], vsplit[face(2 + f), :]).astype(BF16)
        for f in (WEST, EAST, NORTH, SOUTH):
            both = dot32(a_high[face(f), :], u_split[...])
            z = dot32(a_low[face(f), :], u_split[:, 0:nc])
            z = z + both[:, 0:nc] + both[:, nc : 2 * nc]
            if f >= 2:
                high, low = split(z)
                z = dot32(perm_back[f - 2], high) + dot32(perm_back[f - 2], low)
            outbox[r, f] = z

            @pl.when(exists[f])
            def _():
                face_copy(r, f).start()

            if f == EAST:
                between()

    def face_arrived(r, f):
        g = OPPOSITE[f]

        @pl.when(exists[f])
        def _():
            remote(
                outbox.at[r, g], inbox.at[r, f], face_send.at[r, g], face_recv.at[r, f], place[f]
            ).wait_recv()

    def apply_finish(r, out):
        for f in (EAST, WEST, SOUTH, NORTH):
            face_arrived(r, f)
            delta = outbox[r, f] - inbox[r, f] if f < 2 else inbox[r, f] - outbox[r, f]
            out[face(f), :] = delta * free4[face(f), :]

    def solve(r):
        c = terms[r, :, :, 0:8, :].reshape(nx * ny * 8, nc)
        full = inverse[...].reshape(nx * ny * 8, wide)
        alpha = jnp.dot(
            full, c, precision=lax.Precision.HIGHEST, preferred_element_type=F32
        )
        alphas[...] = alpha.reshape(nx * ny, 8, nc)
        fill(0, me_x, me_y)
        for f in range(4):
            fill(f + 1, *place[f])
        return jnp.sum(c * alpha, axis=0, keepdims=True)

    def fill(which, x, y):
        for k, (dx, dy) in enumerate(((0, 0), (0, 1), (1, 0), (0, -1), (-1, 0))):
            xx = jnp.clip(x + dx, 0, nx - 1)
            yy = jnp.clip(y + dy, 0, ny - 1)
            high, low = split(alphas[xx * ny + yy])
            alpha_pair[which, 8 * k : 8 * k + 8, 0:nc] = high.astype(F32)
            alpha_pair[which, 8 * k : 8 * k + 8, nc : 2 * nc] = low.astype(F32)

    def product(left_high, left_low, right):
        both = dot32(left_high, right)
        return dot32(left_low, right[:, 0:nc]) + both[:, 0:nc] + both[:, nc : 2 * nc]

    def mode_image(f):
        return product(
            g_high[face(f), :], g_low[face(f), :], alpha_pair[0].astype(BF16)
        )

    def dual_mode_image(f):
        right = jnp.concatenate([alpha_pair[0], alpha_pair[f + 1]], axis=0).astype(BF16)
        return product(fg_high[face(f), :], fg_low[face(f), :], right)

    def own_sum(left, right):
        return jnp.sum(
            left[0 : 2 * lf, :] * right[0 : 2 * lf, :], axis=0, keepdims=True
        )

    def totals(r, rows):
        return jnp.sum(terms[r, :, :, 0:rows, :].reshape(nx * ny, rows, nc), axis=0)

    alpha_pair[...] = jnp.zeros_like(alpha_pair)

    vsplit[:, 0:nc] = g_high[...]
    vsplit[:, nc : 2 * nc] = g_low[...]
    apply_start(0, lambda: None)
    finish(rhs_row)
    finish(inv_row)
    solve(0)
    for f in range(2):
        mult_ref[face(f), :] = mode_image(f)
    for f in (EAST, WEST, SOUTH, NORTH):
        face_arrived(0, f)
        sign = 1.0 if f < 2 else -1.0
        mask = free4[face(f), :] * sign
        for half, values in enumerate((outbox[0, f] * mask, -inbox[0, f] * mask)):
            high, low = split(values)
            fg_high[face(f), half * nc : (half + 1) * nc] = high
            fg_low[face(f), half * nc : (half + 1) * nc] = low

    l_copy.wait()
    for f in range(2):
        @pl.when(exists[2 + f])
        def _():
            neighbour_copy(
                f, loads_hbm.at[face(f)], loads4.at[face(2 + f)], ld_send.at[f], ld_recv.at[f]
            ).wait_recv()
    for f in range(4):
        p_f[face(f), :] = dual_mode_image(f) - loads4[face(f), :] * free4[face(f), :]

    def spread_terms(r, rows):
        mine = terms.at[r, me_x, me_y, pl.ds(0, rows)]
        for tx in range(nx):
            for ty in range(ny):
                if tx or ty:
                    remote(
                        mine, mine, t_send.at[r], t_recv.at[r],
                        (lax.rem(me_x + tx, nx), lax.rem(me_y + ty, ny)),
                    ).start()

    def all_terms(r, rows):
        every = terms.at[r].reshape(nx * ny, 16, nc).at[pl.ds(0, others), pl.ds(0, rows)]
        return remote(every, every, t_send.at[r], t_recv.at[r], (me_x, lax.rem(me_y + 1, ny)))

    def round_trip(r, rows, apply, out):
        spread_terms(r, rows)
        if apply:
            apply_start(r, lambda: None)
        all_terms(r, rows).wait_recv()
        inner = solve(r)
        if apply:
            apply_finish(r, out)
        return inner

    split_field(p_f)
    coarse_terms(1)
    round_trip(1, 8, True, q_f)
    for f in range(4):
        p = p_f[face(f), :] - mode_image(f)
        p_f[face(f), :] = p
        d_f[face(f), :] = p
        q = q_f[face(f), :] - dual_mode_image(f)
        q_f[face(f), :] = q
        fp_f[face(f), :] = q

    norm = None
    for step in range(ITERS):
        r = step + 2
        last = step + 1 == ITERS
        split_field(q_f)
        coarse_terms(r)
        rows = 8 if last else 9
        terms[r, me_x, me_y, 6:7, :] = own_sum(d_f, q_f)
        if not last:
            terms[r, me_x, me_y, 7:8, :] = own_sum(p_f, p_f if step == 0 else q_f)
            terms[r, me_x, me_y, 8:9, :] = own_sum(q_f, q_f)
        inner = round_trip(r, rows, not last, fq_f)
        total = totals(r, rows)
        curvature = total[6:7, :]
        if step == 0:
            norm = total[7:8, :]
            cross = curvature
        else:
            cross = total[7:8, :]
        size = norm / curvature
        mult_ref[...] = mult_ref[...] + size * d_f[0 : 2 * lf, :]
        if last:
            for f in range(2):
                proj_ref[face(f), :] = p_f[face(f), :] + size * (q_f[face(f), :] - mode_image(f))
            break
        norm_next = norm + 2.0 * size * cross + size * size * (total[8:9, :] - inner)
        ratio = norm_next / norm
        for f in range(4):
            q = q_f[face(f), :]
            p = p_f[face(f), :] + size * (q - mode_image(f))
            p_f[face(f), :] = p
            fp = fp_f[face(f), :] + size * (fq_f[face(f), :] - dual_mode_image(f))
            fp_f[face(f), :] = fp
            d_f[face(f), :] = p + ratio * d_f[face(f), :]
            q_f[face(f), :] = fp + ratio * q
        norm = norm_next

    for r in range(1, ROUNDS):
        all_terms(r, 8 if r in (1, ROUNDS - 1) else 9).wait_send()
    for copy in pending:
        copy.wait_send()
    for f in range(2):
        @pl.when(exists[f])
        def _():
            neighbour_copy(f, pack.at[f], nb_pack.at[f], pk_send.at[f], pk_recv.at[f]).wait_send()
            neighbour_copy(
                f, loads_hbm.at[face(f)], loads4.at[face(2 + f)], ld_send.at[f], ld_recv.at[f]
            ).wait_send()
    for f in range(4):
        @pl.when(exists[f])
        def _():
            for r in range(APPLIES):
                face_copy(r, f).wait_send()


def solution(mesh):
    nx, ny = mesh.shape["gx"], mesh.shape["gy"]

    def local(dual_ops, loads, coarse_rhs, coarse_modes, free_mask, face_match, coarse_rows):
        lm = dual_ops.shape[-1]
        lf, nc = loads.shape[-2:]
        wide = nx * ny * 8
        vmem = pl.BlockSpec(memory_space=pltpu.VMEM)
        hbm = pl.BlockSpec(memory_space=pl.ANY)
        dma = pltpu.SemaphoreType.DMA
        out = jax.ShapeDtypeStruct((2 * lf, nc), F32)
        field = pltpu.VMEM((lm, nc), F32)
        mult, proj = pl.pallas_call(
            functools.partial(kernel, nx, ny),
            out_shape=(out, out),
            in_specs=[hbm, hbm] + [vmem] * 5,
            out_specs=(vmem, vmem),
            scratch_shapes=[
                pltpu.VMEM((lm, lm), F32),
                pltpu.VMEM((lm, lm), BF16),
                pltpu.VMEM((lm, lm), BF16),
                field,
                pltpu.VMEM((2, 24, lf), F32),
                pltpu.VMEM((2, 24, lf), F32),
                pltpu.VMEM((nx, ny, 8, wide), F32),
                pltpu.VMEM((ROUNDS, nx, ny, 16, nc), F32),
                pltpu.VMEM((nx * ny, 8, nc), F32),
                pltpu.VMEM((5, nc, 2 * nc), F32),
                pltpu.VMEM((16, lm), F32),
                pltpu.VMEM((lm, nc), BF16),
                pltpu.VMEM((lm, nc), BF16),
                pltpu.VMEM((lm, 2 * nc), BF16),
                pltpu.VMEM((lm, 2 * nc), BF16),
                field,
                pltpu.VMEM((nc, lf), F32),
                pltpu.VMEM((2, lf, lf), BF16),
                pltpu.VMEM((2, lf, lf), BF16),
                pltpu.VMEM((lm, 2 * nc), BF16),
                pltpu.VMEM((lm, 2 * nc), BF16),
                pltpu.VMEM((APPLIES, 4, lf, nc), F32),
                pltpu.VMEM((APPLIES, 4, lf, nc), F32),
                field, field, field, field, field,
                dma((6,)),
                dma,
                dma((APPLIES, 4)),
                dma((APPLIES, 4)),
                dma((2,)), dma((2,)), dma((2,)), dma((2,)),
                dma((ny,)), dma((ny,)),
                dma((nx,)), dma((nx,)),
                dma((ny,)), dma((ny,)), dma((nx,)), dma((nx,)),
                dma((ROUNDS,)), dma((ROUNDS,)),
            ],
            compiler_params=pltpu.CompilerParams(
                collective_id=0, has_side_effects=True, vmem_limit_bytes=58 * 1024 * 1024
            ),
        )(
            dual_ops.reshape(lm, lm),
            loads.reshape(2 * lf, nc),
            coarse_rhs.reshape(coarse_rhs.shape[2], 1, nc),
            jnp.swapaxes(coarse_modes.reshape(coarse_modes.shape[2:]), 1, 2),
            free_mask.reshape(free_mask.shape[2:]),
            face_match.reshape(face_match.shape[2:]),
            coarse_rows.reshape(-1, 1, coarse_rows.shape[-1]),
        )
        return (mult.reshape(1, 1, 2, lf, nc), proj.reshape(1, 1, 2, lf, nc))

    in_specs = (
        P("gx", "gy", None, None),
        P("gx", "gy", None, None, None),
        P("gx", "gy", None, None),
        P("gx", "gy", None, None, None, None),
        P("gx", "gy", None, None),
        P("gx", "gy", None, None),
        P("gx", "gy", None, None, None),
    )
    out_specs = (P("gx", "gy", None, None, None), P("gx", "gy", None, None, None))
    return jax.shard_map(local, mesh=mesh, in_specs=in_specs, out_specs=out_specs, check_vma=False)
```

```python
import functools

import jax
import jax.numpy as jnp
from jax import lax
from jax.experimental import pallas as pl
from jax.experimental.pallas import tpu as pltpu
from jax.sharding import PartitionSpec as P

ITERS = 3
F32 = jnp.float32
BF16 = jnp.bfloat16
MESH = pl.DeviceIdType.MESH
EAST, SOUTH, WEST, NORTH = 0, 1, 2, 3
OPPOSITE = (WEST, NORTH, EAST, SOUTH)
ROUNDS = ITERS + 2
APPLIES = ITERS + 1
PIECES = 4
AROUND = ((0, 0), (0, 1), (1, 0), (0, -1), (-1, 0))


def split(values):
    high = values.astype(BF16)
    low = (values - high.astype(F32)).astype(BF16)
    return high, low


def split3(values):
    high = values.astype(BF16)
    rest = values - high.astype(F32)
    mid, low = split(rest)
    return high, mid, low


def dot32(left, right):
    return jnp.dot(left, right, preferred_element_type=F32)


def rows_of(*parts):
    return jnp.concatenate(parts, axis=0)


def beside(*parts):
    return jnp.concatenate(parts, axis=1)


def kernel(
    nx, ny, a_hbm, loads_hbm, rhs_ref, modes_ref, free_ref, match_ref, rows_ref,
    mult_ref, proj_ref,
    a_stage, a_high, a_low, loads4, pack, nb_pack, mpack, nb_match, inverse, inv_parts, terms, alphas,
    alpha_cat, gt8, gtb, images, free4, put, swap, vsplit, fold_out, fold_in, outbox, inbox,
    p_f, d_f, q_f, fp_f,
    a_sem, l_sem, face_send, face_recv, fold_send, fold_recv, pk_send, pk_recv, mp_send, mp_recv,
    ld_send, ld_recv, gy_send, gy_recv, gx_send, gx_recv, cy_send, cy_recv, cx_send, cx_recv,
    t_send, t_recv,
):
    lf = free_ref.shape[1]
    nc = mult_ref.shape[1]
    lm = a_high.shape[0]
    modes = rhs_ref.shape[0]
    ncoarse = rows_ref.shape[2]
    wide = inverse.shape[3]
    others = nx * ny - 1
    h = lf // PIECES
    lane_step = nc // PIECES
    half = nc // 2
    me_x = lax.axis_index("gx")
    me_y = lax.axis_index("gy")
    exists = (me_y < ny - 1, me_x < nx - 1, me_y > 0, me_x > 0)
    place = ((me_x, me_y + 1), (me_x + 1, me_y), (me_x, me_y - 1), (me_x - 1, me_y))

    def face(f):
        return pl.ds(f * lf, lf)

    def piece(f, b):
        return pl.ds(f * lf + b * h, h)

    chunks = 2 * PIECES
    chunk = lm // chunks
    a_copies = [
        pltpu.make_async_copy(
            a_hbm.at[pl.ds(i * chunk, chunk)], a_stage.at[pl.ds(i * chunk, chunk)], a_sem.at[i]
        )
        for i in range(chunks)
    ]
    for copy in a_copies:
        copy.start()
    l_copy = pltpu.make_async_copy(loads_hbm, loads4.at[pl.ds(0, 2 * lf)], l_sem)
    l_copy.start()

    barrier = pltpu.get_barrier_semaphore()
    for t in range(1, nx):
        pl.semaphore_signal(
            barrier, inc=1, device_id=(lax.rem(me_x + t, nx), me_y), device_id_type=MESH
        )
    for t in range(1, ny):
        pl.semaphore_signal(
            barrier, inc=1, device_id=(me_x, lax.rem(me_y + t, ny)), device_id_type=MESH
        )

    pack[...] = jnp.zeros_like(pack)
    mpack[...] = jnp.zeros_like(mpack)
    for f in range(2):
        pack[f, 0:modes, :] = modes_ref[f, :, 0, :]
        pack[f, 8 : 8 + modes, :] = modes_ref[f, :, 1, :]
        pack[f, 16:17, :] = free_ref[f : f + 1, :].astype(F32)
        mpack[f, 0:1, :] = match_ref[f : f + 1, :].astype(F32)

    row = lax.broadcasted_iota(jnp.int32, (ncoarse, wide), 0)
    col = lax.broadcasted_iota(jnp.int32, (ncoarse, wide), 1)
    slot = jnp.bitwise_and(col, 7)
    spread = jnp.where((row == modes * jnp.right_shift(col, 3) + slot) & (slot < modes), 1.0, 0.0)
    inverse[me_x, me_y] = jnp.zeros((8, wide), F32)
    inverse[me_x, me_y, 0:modes, :] = jnp.dot(
        rows_ref[0:modes, 0, :], spread.astype(F32), precision=lax.Precision.HIGHEST,
        preferred_element_type=F32,
    )
    terms[0, me_x, me_y] = jnp.zeros((16, nc), F32)
    terms[0, me_x, me_y, 0:modes, :] = rhs_ref[:, 0, :]

    pl.semaphore_wait(barrier, nx + ny - 2)

    def remote(src, dst, send, recv, where):
        return pltpu.make_async_remote_copy(
            src_ref=src, dst_ref=dst, send_sem=send, recv_sem=recv,
            device_id=where, device_id_type=MESH,
        )

    def to_owned(f):
        return remote(pack.at[f], nb_pack.at[f], pk_send.at[f], pk_recv.at[f], place[f])

    def to_owner(f):
        return remote(mpack.at[f], nb_match.at[f], mp_send.at[f], mp_recv.at[f], place[2 + f])

    def loads_copy(f):
        return remote(
            loads_hbm.at[face(f)], loads4.at[face(2 + f)], ld_send.at[f], ld_recv.at[f], place[f]
        )

    for f in range(2):
        @pl.when(exists[f])
        def _():
            to_owned(f).start()

        @pl.when(exists[2 + f])
        def _():
            to_owner(f).start()

    def spread_column(view, send, recv):
        copies = []
        for t in range(1, ny):
            copies.append(remote(
                view(me_x, me_y), view(me_x, me_y), send.at[t], recv.at[t],
                (me_x, lax.rem(me_y + t, ny)),
            ))
        return copies

    def spread_row(view, send, recv):
        copies = []
        for t in range(1, nx):
            copies.append(remote(
                view(me_x), view(me_x), send.at[t], recv.at[t],
                (lax.rem(me_x + t, nx), me_y),
            ))
        return copies

    pending = []

    def begin(copies):
        for copy in copies:
            copy.start()
        pending.extend(copies)

    def finish(copies):
        for copy in copies:
            copy.wait_recv()

    inv_col = spread_column(lambda x, y: inverse.at[x, y], cy_send, cy_recv)
    inv_row = spread_row(lambda x: inverse.at[x], cx_send, cx_recv)
    rhs_col = spread_column(lambda x, y: terms.at[0, x, y, pl.ds(0, 8)], gy_send, gy_recv)
    rhs_row = spread_row(lambda x: terms.at[0, x, :, pl.ds(0, 8)], gx_send, gx_recv)
    begin(rhs_col)
    begin(inv_col)

    for f in range(4):
        @pl.when(jnp.logical_not(exists[f]))
        def _():
            fold_in[f] = jnp.zeros((h, nc), F32)
            for r in range(1, APPLIES):
                inbox[r - 1, f] = jnp.zeros((lf, nc), F32)
    for f in range(2):
        @pl.when(jnp.logical_not(exists[f]))
        def _():
            nb_match[f] = jnp.zeros((8, lf), F32)

        @pl.when(jnp.logical_not(exists[2 + f]))
        def _():
            nb_pack[f] = jnp.zeros((24, lf), F32)
            loads4[face(2 + f), :] = jnp.zeros((lf, nc), F32)

    def cast_chunk(i):
        a_copies[i].wait()
        for t in range(2):
            f, b = divmod(2 * i + t, PIECES)
            high, low = split(a_stage[piece(f, b), :])
            to = pl.ds((b * 4 + f) * h, h)
            a_high[to, :] = high
            a_low[to, :] = low

    for i in range(chunks // 2):
        cast_chunk(i)

    finish(rhs_col)
    begin(rhs_row)
    finish(inv_col)
    begin(inv_row)
    for f in range(2):
        @pl.when(exists[f])
        def _():
            loads_copy(f).start()

    for i in range(chunks // 2, chunks):
        cast_chunk(i)

    slots = lax.broadcasted_iota(jnp.int32, (lf, lf), 0)
    backs = []
    for f in range(2):
        back = jnp.where(slots == match_ref[f : f + 1, :], 1.0, 0.0).astype(F32)
        swap[2 + f] = (-jnp.transpose(back)).astype(BF16)
        backs.append(back.astype(BF16))

    for f in range(2):
        @pl.when(exists[2 + f])
        def _():
            to_owned(f).wait_recv()

    def prepare(f):
        if f < 2:
            mask = pack[f, 16:17, :]
            owner = pack[f, 0:8, :] * mask
            other = pack[f, 8:16, :] * mask
            own_part, far_part = owner, other
        else:
            high, low = split(nb_pack[f - 2])
            local = dot32(high, backs[f - 2]) + dot32(low, backs[f - 2])
            mask = local[16:17, :]
            own_part = -local[8:16, :] * mask
            far_part = -local[0:8, :] * mask
        put[...] = jnp.zeros_like(put)
        put[0:modes, :] = own_part[0:modes, :]
        put[modes * (f + 1) : modes * (f + 2), :] = far_part[0:modes, :]
        high, low = split(own_part)
        gt8[0:8, face(f)] = high.astype(F32)
        gt8[8:16, face(f)] = low.astype(F32)
        high, low = split(jnp.transpose(put[...]))
        vsplit[face(f), 0:nc] = high
        vsplit[face(f), nc : 2 * nc] = low
        if f < 2:
            images[f, pl.ds(lf, lf), :] = (
                high.astype(F32) + pltpu.roll(low.astype(F32), half, 1)
            ).astype(BF16)
        free4[face(f), :] = jnp.transpose(jnp.broadcast_to(mask, (nc, lf)))

    for f in range(4):
        prepare(f)
    gtb[...] = gt8[...].astype(BF16)

    def face_copy(r, f, b):
        g = OPPOSITE[f]
        part = pl.ds(b * h, h)
        return remote(
            outbox.at[r - 1, f, part], inbox.at[r - 1, g, part],
            face_send.at[f], face_recv.at[r - 1, g], place[f],
        )

    def block(b):
        at = pl.ds(b * 4 * h, 4 * h)
        both = dot32(a_high[at, :], vsplit[...])
        z = dot32(a_low[at, :], vsplit[:, 0:nc])
        return z + both[:, 0:nc] + both[:, nc : 2 * nc]

    def apply_start(r):
        for b in range(PIECES):
            z = block(b)
            for f in range(4):
                outbox[r - 1, f, pl.ds(b * h, h), :] = z[f * h : (f + 1) * h, :]
            for f in (WEST, EAST, NORTH, SOUTH):
                @pl.when(exists[f])
                def _():
                    face_copy(r, f, b).start()

    def face_arrived(r, f):
        g = OPPOSITE[f]

        @pl.when(exists[f])
        def _():
            remote(
                outbox.at[r - 1, g], inbox.at[r - 1, f], face_send.at[g], face_recv.at[r - 1, f],
                place[f],
            ).wait_recv()

    def exchanged(f, values):
        high, low = split(values)
        both = dot32(swap[f], beside(high, low))
        return both[:, 0:nc] + both[:, nc : 2 * nc]

    def fold_copy(f):
        g = OPPOSITE[f]
        return remote(
            fold_out.at[f], fold_in.at[g], fold_send.at[f], fold_recv.at[g], place[f]
        )

    for b in range(PIECES):
        z = block(b)
        for f in range(4):
            part = z[f * h : (f + 1) * h, :]
            fp_f[piece(f, b), :] = part
            if b == 0:
                fold_out[f] = part
            else:
                fold_out[f] = fold_out[f] + pltpu.roll(part, b * lane_step, 1)
    for f in (WEST, EAST, NORTH, SOUTH):
        @pl.when(exists[f])
        def _():
            fold_copy(f).start()

    for f in range(2):
        @pl.when(exists[f])
        def _():
            remote(
                mpack.at[f], nb_match.at[f], mp_send.at[f], mp_recv.at[f], place[f]
            ).wait_recv()

        back = jnp.where(slots == nb_match[f, 0:1, :].astype(jnp.int32), -1.0, 0.0)
        swap[f] = back.astype(BF16)

    alpha_cat[...] = jnp.zeros_like(alpha_cat)
    finish(rhs_row)
    finish(inv_row)
    high, mid, low = split3(inverse[...].reshape(nx * ny * 8, wide))
    inv_parts[:, 0:wide] = high
    inv_parts[:, wide : 2 * wide] = mid
    inv_parts[:, 2 * wide : 3 * wide] = low
    inv_parts[:, 3 * wide : 4 * wide] = high

    def coarse_terms(r):
        both = dot32(gtb[...], vsplit[...])
        terms[r, me_x, me_y, 0:8, :] = (
            both[0:8, 0:nc] + both[0:8, nc : 2 * nc] + both[8:16, 0:nc]
        )

    def solve(r):
        c = terms[r, :, :, 0:8, :].reshape(nx * ny * 8, nc)
        high, mid, low = split3(c)
        nothing = jnp.zeros_like(high)
        right = rows_of(
            beside(high, mid), beside(high, mid), beside(high, nothing), beside(low, nothing)
        )
        both = dot32(inv_parts[...], right)
        alpha = both[:, 0:nc] + both[:, nc : 2 * nc]
        alphas[...] = alpha.reshape(nx * ny, 8, nc)
        return jnp.sum(c * alpha, axis=0, keepdims=True)

    def gather_alpha():
        for which in range(5):
            x, y = (me_x, me_y) if which == 0 else place[which - 1]
            for k, (dx, dy) in enumerate(AROUND):
                xx = jnp.clip(x + dx, 0, nx - 1)
                yy = jnp.clip(y + dy, 0, ny - 1)
                values = alphas[xx * ny + yy][0:modes, :]
                if which == 0:
                    for f in range(4):
                        alpha_cat[f, modes * k : modes * (k + 1), :] = values
                else:
                    alpha_cat[
                        which - 1, lane_step + modes * k : lane_step + modes * (k + 1), :
                    ] = values

    def right_side(f):
        high, low = split(alpha_cat[f])
        return rows_of(beside(high, low), beside(high, jnp.zeros_like(high)))

    def dual_mode_image(f):
        both = dot32(images[f, pl.ds(0, lf), :], right_side(f))
        return both[:, 0:nc] + both[:, nc : 2 * nc]

    def mode_image(f):
        both = dot32(images[f, pl.ds(lf, lf), :], right_side(f))
        return both[:, 0:nc] + both[:, nc : 2 * nc]

    def own_sum(left, right):
        return jnp.sum(
            left[0 : 2 * lf, :] * right[0 : 2 * lf, :], axis=0, keepdims=True
        )

    def spread_terms(r, rows):
        mine = terms.at[r, me_x, me_y, pl.ds(0, rows)]
        for tx in range(nx):
            for ty in range(ny):
                if tx or ty:
                    remote(
                        mine, mine, t_send.at[r], t_recv.at[r],
                        (lax.rem(me_x + tx, nx), lax.rem(me_y + ty, ny)),
                    ).start()

    def all_terms(r, rows):
        every = terms.at[r].reshape(nx * ny, 16, nc).at[pl.ds(0, others), pl.ds(0, rows)]
        return remote(every, every, t_send.at[r], t_recv.at[r], (me_x, lax.rem(me_y + 1, ny)))

    def totals(r, rows):
        return jnp.sum(terms[r, :, :, 0:rows, :].reshape(nx * ny, rows, nc), axis=0)

    solve(0)
    gather_alpha()
    for f in range(2):
        mult_ref[face(f), :] = mode_image(f)

    l_copy.wait()
    for f in range(2):
        @pl.when(exists[2 + f])
        def _():
            loads_copy(f).wait_recv()
    for f in range(4):
        values = loads4[face(f), :]
        if f >= 2:
            high, mid, low = split3(values)
            both = dot32(swap[f], beside(high, mid))
            values = both[:, 0:nc] + (both[:, nc : 2 * nc] + dot32(swap[f], low))
        loads4[face(f), :] = values * free4[face(f), :]

    lanes = lax.broadcasted_iota(jnp.int32, (h, nc), 1)
    for f in (EAST, WEST, SOUTH, NORTH):
        @pl.when(exists[f])
        def _():
            g = OPPOSITE[f]
            remote(
                fold_out.at[g], fold_in.at[f], fold_send.at[g], fold_recv.at[f], place[f]
            ).wait_recv()

        came = fold_in[f]
        parts = []
        for b in range(PIECES):
            moved = came if b == 0 else pltpu.roll(came, nc - b * lane_step, 1)
            parts.append(jnp.where(lanes < lane_step, moved, 0.0))
        far = exchanged(f, rows_of(*parts))
        values = (fp_f[face(f), :] + pltpu.roll(far, lane_step, 1)) * free4[face(f), :]
        high, low = split(values)
        images[f, pl.ds(0, lf), :] = (
            high.astype(F32) + pltpu.roll(low.astype(F32), half, 1)
        ).astype(BF16)

    def put_field(f, values):
        high, low = split(values)
        vsplit[face(f), 0:nc] = high
        vsplit[face(f), nc : 2 * nc] = low

    for f in range(4):
        v = dual_mode_image(f) - loads4[face(f), :]
        put_field(f, v)
        if f < 2:
            p_f[face(f), :] = v

    coarse_terms(1)
    spread_terms(1, 8)
    apply_start(1)
    all_terms(1, 8).wait_recv()
    solve(1)
    gather_alpha()

    def applied(r, f):
        return free4[face(f), :] * (outbox[r - 1, f] + exchanged(f, inbox[r - 1, f]))

    for f in range(4):
        face_arrived(1, f)
    for f in range(4):
        q = applied(1, f) - dual_mode_image(f)
        q_f[face(f), :] = q
        fp_f[face(f), :] = q
        put_field(f, q)
    for f in range(2):
        p = p_f[face(f), :] - mode_image(f)
        p_f[face(f), :] = p
        d_f[face(f), :] = p

    norm = None
    for step in range(ITERS):
        r = step + 2
        last = step + 1 == ITERS
        rows = 8 if last else 9
        coarse_terms(r)
        terms[r, me_x, me_y, 6:7, :] = own_sum(d_f, q_f)
        if not last:
            terms[r, me_x, me_y, 7:8, :] = own_sum(p_f, p_f if step == 0 else q_f)
            terms[r, me_x, me_y, 8:9, :] = own_sum(q_f, q_f)
        spread_terms(r, rows)
        if not last:
            apply_start(r)
        all_terms(r, rows).wait_recv()
        inner = solve(r)
        gather_alpha()
        total = totals(r, rows)
        curvature = total[6:7, :]
        if step == 0:
            norm = total[7:8, :]
            cross = curvature
        else:
            cross = total[7:8, :]
        size = norm / curvature
        if last:
            mult_ref[...] = mult_ref[...] + size * d_f[...]
            for f in range(2):
                proj_ref[face(f), :] = p_f[face(f), :] + size * (q_f[face(f), :] - mode_image(f))
            break
        norm_next = norm + 2.0 * size * cross + size * size * (total[8:9, :] - inner)
        ratio = norm_next / norm
        for f in range(4):
            face_arrived(r, f)
        for f in range(2):
            p_f[face(f), :] = p_f[face(f), :] + size * (q_f[face(f), :] - mode_image(f))
        mult_ref[...] = mult_ref[...] + size * d_f[...]
        for f in range(4):
            fp = fp_f[face(f), :] + size * (applied(r, f) - dual_mode_image(f))
            fp_f[face(f), :] = fp
            q = fp + ratio * q_f[face(f), :]
            q_f[face(f), :] = q
            put_field(f, q)
        d_f[...] = p_f[...] + ratio * d_f[...]
        norm = norm_next

    for r in range(1, ROUNDS):
        all_terms(r, 8 if r in (1, ROUNDS - 1) else 9).wait_send()
    for copy in pending:
        copy.wait_send()
    for f in range(2):
        @pl.when(exists[f])
        def _():
            to_owned(f).wait_send()
            loads_copy(f).wait_send()

        @pl.when(exists[2 + f])
        def _():
            to_owner(f).wait_send()
    for f in range(4):
        @pl.when(exists[f])
        def _():
            fold_copy(f).wait_send()
            remote(
                outbox.at[:, f], inbox.at[:, f], face_send.at[f], face_recv.at[0, f], place[f]
            ).wait_send()


def solution(mesh):
    nx, ny = mesh.shape["gx"], mesh.shape["gy"]

    def local(dual_ops, loads, coarse_rhs, coarse_modes, free_mask, face_match, coarse_rows):
        lm = dual_ops.shape[-1]
        lf, nc = loads.shape[-2:]
        wide = nx * ny * 8
        vmem = pl.BlockSpec(memory_space=pltpu.VMEM)
        hbm = pl.BlockSpec(memory_space=pl.ANY)
        dma = pltpu.SemaphoreType.DMA
        out = jax.ShapeDtypeStruct((2 * lf, nc), F32)
        field = pltpu.VMEM((lm, nc), F32)
        own = pltpu.VMEM((2 * lf, nc), F32)
        mult, proj = pl.pallas_call(
            functools.partial(kernel, nx, ny),
            out_shape=(pltpu.VMEM((2 * lf, nc), F32),) * 2,
            in_specs=[hbm, hbm] + [vmem] * 5,
            out_specs=(vmem, vmem),
            scratch_shapes=[
                pltpu.VMEM((lm, lm), F32),
                pltpu.VMEM((lm, lm), BF16),
                pltpu.VMEM((lm, lm), BF16),
                field,
                pltpu.VMEM((2, 24, lf), F32),
                pltpu.VMEM((2, 24, lf), F32),
                pltpu.VMEM((2, 8, lf), F32),
                pltpu.VMEM((2, 8, lf), F32),
                pltpu.VMEM((nx, ny, 8, wide), F32),
                pltpu.VMEM((wide, 4 * wide), BF16),
                pltpu.VMEM((ROUNDS, nx, ny, 16, nc), F32),
                pltpu.VMEM((nx * ny, 8, nc), F32),
                pltpu.VMEM((4, nc // 2, nc), F32),
                pltpu.VMEM((16, lm), F32),
                pltpu.VMEM((16, lm), BF16),
                pltpu.VMEM((4, 2 * lf, nc), BF16),
                field,
                pltpu.VMEM((nc, lf), F32),
                pltpu.VMEM((4, lf, lf), BF16),
                pltpu.VMEM((lm, 2 * nc), BF16),
                pltpu.VMEM((4, lf // PIECES, nc), F32),
                pltpu.VMEM((4, lf // PIECES, nc), F32),
                pltpu.VMEM((APPLIES - 1, 4, lf, nc), F32),
                pltpu.VMEM((APPLIES - 1, 4, lf, nc), F32),
                own, own, field, field,
                dma((2 * PIECES,)),
                dma,
                dma((4,)),
                dma((APPLIES - 1, 4)),
                dma((4,)), dma((4,)),
                dma((2,)), dma((2,)), dma((2,)), dma((2,)), dma((2,)), dma((2,)),
                dma((ny,)), dma((ny,)), dma((nx,)), dma((nx,)),
                dma((ny,)), dma((ny,)), dma((nx,)), dma((nx,)),
                dma((ROUNDS,)), dma((ROUNDS,)),
            ],
            compiler_params=pltpu.CompilerParams(
                collective_id=0, has_side_effects=True, vmem_limit_bytes=60 * 1024 * 1024
            ),
        )(
            dual_ops.reshape(lm, lm),
            loads.reshape(2 * lf, nc),
            coarse_rhs.reshape(coarse_rhs.shape[2], 1, nc),
            jnp.swapaxes(coarse_modes.reshape(coarse_modes.shape[2:]), 1, 2),
            free_mask.reshape(free_mask.shape[2:]),
            face_match.reshape(face_match.shape[2:]),
            coarse_rows.reshape(-1, 1, coarse_rows.shape[-1]),
        )
        return (mult.reshape(1, 1, 2, lf, nc), proj.reshape(1, 1, 2, lf, nc))

    in_specs = (
        P("gx", "gy", None, None),
        P("gx", "gy", None, None, None),
        P("gx", "gy", None, None),
        P("gx", "gy", None, None, None, None),
        P("gx", "gy", None, None),
        P("gx", "gy", None, None),
        P("gx", "gy", None, None, None),
    )
    out_specs = (P("gx", "gy", None, None, None), P("gx", "gy", None, None, None))
    return jax.shard_map(local, mesh=mesh, in_specs=in_specs, out_specs=out_specs, check_vma=False)
```

```python
import functools

import jax
import jax.numpy as jnp
from jax import lax
from jax.experimental import pallas as pl
from jax.experimental.pallas import tpu as pltpu
from jax.sharding import PartitionSpec as P

ITERS = 3
F32 = jnp.float32
BF16 = jnp.bfloat16
MESH = pl.DeviceIdType.MESH
EAST, SOUTH, WEST, NORTH = 0, 1, 2, 3
OPPOSITE = (WEST, NORTH, EAST, SOUTH)
ROUNDS = ITERS + 2
APPLIES = ITERS + 1
PIECES = 4
ROW_AFTER = 1
AROUND = ((0, 0), (0, 1), (1, 0), (0, -1), (-1, 0))


def split(values):
    high = values.astype(BF16)
    low = (values - high.astype(F32)).astype(BF16)
    return high, low


def split3(values):
    high = values.astype(BF16)
    rest = values - high.astype(F32)
    mid, low = split(rest)
    return high, mid, low


def dot32(left, right):
    return jnp.dot(left, right, preferred_element_type=F32)


def rows_of(*parts):
    return jnp.concatenate(parts, axis=0)


def beside(*parts):
    return jnp.concatenate(parts, axis=1)


def kernel(
    nx, ny, a_hbm, loads_hbm, rhs_ref, modes_ref, free_ref, match_ref, rows_ref,
    mult_ref, proj_ref,
    a_stage, a_high, a_low, loads4, pack, nb_pack, mpack, nb_match, inverse, inv_parts, terms, alphas,
    alpha_cat, gt8, gtb, images, free4, put, swap, vsplit, fold_out, fold_in, outbox, inbox,
    p_f, d_f, q_f, fp_f,
    a_sem, l_sem, face_send, face_recv, fold_send, fold_recv, pk_send, pk_recv, mp_send, mp_recv,
    ld_send, ld_recv, gy_send, gy_recv, gx_send, gx_recv, cy_send, cy_recv, cx_send, cx_recv,
    t_send, t_recv, x_send, x_recv,
):
    lf = free_ref.shape[1]
    nc = mult_ref.shape[1]
    lm = a_high.shape[0]
    modes = rhs_ref.shape[0]
    ncoarse = rows_ref.shape[2]
    wide = inverse.shape[3]
    halves = terms.shape[2]
    others = nx * ny // halves - 1
    h = lf // PIECES
    lane_step = nc // PIECES
    half = nc // 2
    me_x = lax.axis_index("gx")
    me_y = lax.axis_index("gy")
    me_h, side = me_x // halves, lax.rem(me_x, halves)
    exists = (me_y < ny - 1, me_x < nx - 1, me_y > 0, me_x > 0)
    place = ((me_x, me_y + 1), (me_x + 1, me_y), (me_x, me_y - 1), (me_x - 1, me_y))

    def face(f):
        return pl.ds(f * lf, lf)

    def piece(f, b):
        return pl.ds(f * lf + b * h, h)

    chunks = 2 * PIECES
    chunk = lm // chunks
    a_copies = [
        pltpu.make_async_copy(
            a_hbm.at[pl.ds(i * chunk, chunk)], a_stage.at[pl.ds(i * chunk, chunk)], a_sem.at[i]
        )
        for i in range(chunks)
    ]
    for copy in a_copies:
        copy.start()
    l_copy = pltpu.make_async_copy(loads_hbm, loads4.at[pl.ds(0, 2 * lf)], l_sem)
    l_copy.start()

    barrier = pltpu.get_barrier_semaphore()
    for t in range(1, nx):
        pl.semaphore_signal(
            barrier, inc=1, device_id=(lax.rem(me_x + t, nx), me_y), device_id_type=MESH
        )
    for t in range(1, ny):
        pl.semaphore_signal(
            barrier, inc=1, device_id=(me_x, lax.rem(me_y + t, ny)), device_id_type=MESH
        )

    pack[...] = jnp.zeros_like(pack)
    mpack[...] = jnp.zeros_like(mpack)
    for f in range(2):
        pack[f, 0:modes, :] = modes_ref[f, :, 0, :]
        pack[f, 8 : 8 + modes, :] = modes_ref[f, :, 1, :]
        pack[f, 16:17, :] = free_ref[f : f + 1, :].astype(F32)
        mpack[f, 0:1, :] = match_ref[f : f + 1, :].astype(F32)

    row = lax.broadcasted_iota(jnp.int32, (ncoarse, wide), 0)
    col = lax.broadcasted_iota(jnp.int32, (ncoarse, wide), 1)
    slot = jnp.bitwise_and(col, 7)
    spread = jnp.where((row == modes * jnp.right_shift(col, 3) + slot) & (slot < modes), 1.0, 0.0)
    inverse[me_x, me_y] = jnp.zeros((8, wide), F32)
    inverse[me_x, me_y, 0:modes, :] = jnp.dot(
        rows_ref[0:modes, 0, :], spread.astype(F32), precision=lax.Precision.HIGHEST,
        preferred_element_type=F32,
    )
    terms[0, me_h, side, me_y] = jnp.zeros((16, nc), F32)
    terms[0, me_h, side, me_y, 0:modes, :] = rhs_ref[:, 0, :]

    pl.semaphore_wait(barrier, nx + ny - 2)

    def remote(src, dst, send, recv, where):
        return pltpu.make_async_remote_copy(
            src_ref=src, dst_ref=dst, send_sem=send, recv_sem=recv,
            device_id=where, device_id_type=MESH,
        )

    def to_owned(f):
        return remote(pack.at[f], nb_pack.at[f], pk_send.at[f], pk_recv.at[f], place[f])

    def to_owner(f):
        return remote(mpack.at[f], nb_match.at[f], mp_send.at[f], mp_recv.at[f], place[2 + f])

    def loads_copy(f):
        return remote(
            loads_hbm.at[face(f)], loads4.at[face(2 + f)], ld_send.at[f], ld_recv.at[f], place[f]
        )

    for f in range(2):
        @pl.when(exists[f])
        def _():
            to_owned(f).start()

        @pl.when(exists[2 + f])
        def _():
            to_owner(f).start()

    coarse_stages = (
        (
            lambda n: inverse.at[me_x, pl.ds(0, n)], inverse.at[me_x, me_y], cy_send, cy_recv,
            lambda n: inverse.at[pl.ds(0, n)], inverse.at[me_x], cx_send, cx_recv,
        ),
        (
            lambda n: terms.at[0, 0, 0, pl.ds(0, n), pl.ds(0, 8)],
            terms.at[0, me_h, side, me_y, pl.ds(0, 8)], gy_send, gy_recv,
            lambda n: terms.at[0].reshape(nx, ny, 16, nc).at[pl.ds(0, n), :, pl.ds(0, 8)],
            terms.at[0, me_h, side, :, pl.ds(0, 8)], gx_send, gx_recv,
        ),
    )

    def column_begin():
        for _, mine, send, recv, _, _, _, _ in coarse_stages:
            for t in range(1, ny):
                remote(mine, mine, send, recv, (me_x, lax.rem(me_y + t, ny))).start()

    def column_all(stage):
        view, _, send, recv, _, _, _, _ = stage
        return remote(view(ny - 1), view(ny - 1), send, recv, (me_x, lax.rem(me_y + 1, ny)))

    def row_begin():
        for stage in coarse_stages:
            column_all(stage).wait_recv()
        for _, _, _, _, _, mine, send, recv in coarse_stages:
            for t in range(1, nx):
                remote(mine, mine, send, recv, (lax.rem(me_x + t, nx), me_y)).start()

    def row_all(stage):
        _, _, _, _, view, _, send, recv = stage
        return remote(view(nx - 1), view(nx - 1), send, recv, (lax.rem(me_x + 1, nx), me_y))

    column_begin()
    for f in range(2):
        @pl.when(exists[f])
        def _():
            loads_copy(f).start()

    for f in range(4):
        @pl.when(jnp.logical_not(exists[f]))
        def _():
            fold_in[f] = jnp.zeros((h, nc), F32)
            for r in range(1, APPLIES):
                inbox[r - 1, f] = jnp.zeros((lf, nc), F32)
    for f in range(2):
        @pl.when(jnp.logical_not(exists[f]))
        def _():
            nb_match[f] = jnp.zeros((8, lf), F32)

        @pl.when(jnp.logical_not(exists[2 + f]))
        def _():
            nb_pack[f] = jnp.zeros((24, lf), F32)
            loads4[face(2 + f), :] = jnp.zeros((lf, nc), F32)

    def cast_chunk(i):
        a_copies[i].wait()
        for t in range(2):
            f, b = divmod(2 * i + t, PIECES)
            high, low = split(a_stage[piece(f, b), :])
            to = pl.ds((b * 4 + f) * h, h)
            a_high[to, :] = high
            a_low[to, :] = low

    for i in range(chunks):
        cast_chunk(i)

    slots = lax.broadcasted_iota(jnp.int32, (lf, lf), 0)
    backs = []
    for f in range(2):
        back = jnp.where(slots == match_ref[f : f + 1, :], 1.0, 0.0).astype(F32)
        swap[2 + f] = (-jnp.transpose(back)).astype(BF16)
        backs.append(back.astype(BF16))

    def prepare(f):
        if f < 2:
            mask = pack[f, 16:17, :]
            owner = pack[f, 0:8, :] * mask
            other = pack[f, 8:16, :] * mask
            own_part, far_part = owner, other
        else:
            high, low = split(nb_pack[f - 2])
            local = dot32(high, backs[f - 2]) + dot32(low, backs[f - 2])
            mask = local[16:17, :]
            own_part = -local[8:16, :] * mask
            far_part = -local[0:8, :] * mask
        put[...] = jnp.zeros_like(put)
        put[0:modes, :] = own_part[0:modes, :]
        put[modes * (f + 1) : modes * (f + 2), :] = far_part[0:modes, :]
        high, low = split(own_part)
        gt8[0:8, face(f)] = high.astype(F32)
        gt8[8:16, face(f)] = low.astype(F32)
        high, low = split(jnp.transpose(put[...]))
        vsplit[face(f), 0:nc] = high
        vsplit[face(f), nc : 2 * nc] = low
        if f < 2:
            images[f, pl.ds(lf, lf), :] = (
                high.astype(F32) + pltpu.roll(low.astype(F32), half, 1)
            ).astype(BF16)
        free4[face(f), :] = jnp.transpose(jnp.broadcast_to(mask, (nc, lf)))

    near, far_half = pl.ds(0, 2 * lf), pl.ds(2 * lf, 2 * lf)

    def block_half(b, part):
        at = pl.ds(b * 4 * h, 4 * h)
        both = dot32(a_high[at, part], vsplit[part, :])
        z = dot32(a_low[at, part], vsplit[part, 0:nc])
        return z + both[:, 0:nc] + both[:, nc : 2 * nc]

    for f in range(2):
        prepare(f)
    for b in range(PIECES):
        z = block_half(b, near)
        for f in range(4):
            fp_f[piece(f, b), :] = z[f * h : (f + 1) * h, :]

    for f in range(2):
        @pl.when(exists[2 + f])
        def _():
            to_owned(f).wait_recv()

    for f in range(2, 4):
        prepare(f)
    gtb[...] = gt8[...].astype(BF16)

    def face_copy(r, f, b):
        g = OPPOSITE[f]
        part = pl.ds(b * h, h)
        return remote(
            outbox.at[r - 1, f, part], inbox.at[r - 1, g, part],
            face_send.at[f], face_recv.at[r - 1, g], place[f],
        )

    def block(b):
        at = pl.ds(b * 4 * h, 4 * h)
        both = dot32(a_high[at, :], vsplit[...])
        z = dot32(a_low[at, :], vsplit[:, 0:nc])
        return z + both[:, 0:nc] + both[:, nc : 2 * nc]

    def apply_start(r):
        for b in range(PIECES):
            z = block(b)
            for f in range(4):
                outbox[r - 1, f, pl.ds(b * h, h), :] = z[f * h : (f + 1) * h, :]
            for f in (WEST, EAST, NORTH, SOUTH):
                @pl.when(exists[f])
                def _():
                    face_copy(r, f, b).start()

    def face_arrived(r, f):
        g = OPPOSITE[f]

        @pl.when(exists[f])
        def _():
            remote(
                outbox.at[r - 1, g], inbox.at[r - 1, f], face_send.at[g], face_recv.at[r - 1, f],
                place[f],
            ).wait_recv()

    def exchanged(f, values):
        high, low = split(values)
        both = dot32(swap[f], beside(high, low))
        return both[:, 0:nc] + both[:, nc : 2 * nc]

    def fold_copy(f):
        g = OPPOSITE[f]
        return remote(
            fold_out.at[f], fold_in.at[g], fold_send.at[f], fold_recv.at[g], place[f]
        )

    for b in range(PIECES):
        z = block_half(b, far_half)
        for f in range(4):
            part = fp_f[piece(f, b), :] + z[f * h : (f + 1) * h, :]
            fp_f[piece(f, b), :] = part
            if b == 0:
                fold_out[f] = part
            else:
                fold_out[f] = fold_out[f] + pltpu.roll(part, b * lane_step, 1)
        if b == ROW_AFTER:
            row_begin()
    for f in (WEST, EAST, NORTH, SOUTH):
        @pl.when(exists[f])
        def _():
            fold_copy(f).start()

    for f in range(2):
        @pl.when(exists[f])
        def _():
            remote(
                mpack.at[f], nb_match.at[f], mp_send.at[f], mp_recv.at[f], place[f]
            ).wait_recv()

        back = jnp.where(slots == nb_match[f, 0:1, :].astype(jnp.int32), -1.0, 0.0)
        swap[f] = back.astype(BF16)

    alpha_cat[...] = jnp.zeros_like(alpha_cat)
    for stage in coarse_stages:
        row_all(stage).wait_recv()
    high, mid, low = split3(inverse[...].reshape(nx * ny * 8, wide))
    inv_parts[:, 0:wide] = high
    inv_parts[:, wide : 2 * wide] = mid
    inv_parts[:, 2 * wide : 3 * wide] = low
    inv_parts[:, 3 * wide : 4 * wide] = high

    def coarse_terms(r):
        both = dot32(gtb[...], vsplit[...])
        terms[r, me_h, side, me_y, 0:8, :] = (
            both[0:8, 0:nc] + both[0:8, nc : 2 * nc] + both[8:16, 0:nc]
        )

    def solve(r):
        c = terms[r, :, :, :, 0:8, :].reshape(nx * ny * 8, nc)
        high, mid, low = split3(c)
        nothing = jnp.zeros_like(high)
        right = rows_of(
            beside(high, mid), beside(high, mid), beside(high, nothing), beside(low, nothing)
        )
        both = dot32(inv_parts[...], right)
        alpha = both[:, 0:nc] + both[:, nc : 2 * nc]
        alphas[...] = alpha.reshape(nx * ny, 8, nc)
        return jnp.sum(c * alpha, axis=0, keepdims=True)

    def gather_alpha():
        for which in range(5):
            x, y = (me_x, me_y) if which == 0 else place[which - 1]
            for k, (dx, dy) in enumerate(AROUND):
                xx = jnp.clip(x + dx, 0, nx - 1)
                yy = jnp.clip(y + dy, 0, ny - 1)
                values = alphas[xx * ny + yy][0:modes, :]
                if which == 0:
                    for f in range(4):
                        alpha_cat[f, modes * k : modes * (k + 1), :] = values
                else:
                    alpha_cat[
                        which - 1, lane_step + modes * k : lane_step + modes * (k + 1), :
                    ] = values

    def right_side(f):
        high, low = split(alpha_cat[f])
        return rows_of(beside(high, low), beside(high, jnp.zeros_like(high)))

    def dual_mode_image(f):
        both = dot32(images[f, pl.ds(0, lf), :], right_side(f))
        return both[:, 0:nc] + both[:, nc : 2 * nc]

    def mode_image(f):
        both = dot32(images[f, pl.ds(lf, lf), :], right_side(f))
        return both[:, 0:nc] + both[:, nc : 2 * nc]

    def own_sum(left, right):
        return jnp.sum(
            left[0 : 2 * lf, :] * right[0 : 2 * lf, :], axis=0, keepdims=True
        )

    def spread_terms(r, rows):
        mine = terms.at[r, me_h, side, me_y, pl.ds(0, rows)]
        for tx in range(nx // halves):
            for ty in range(ny):
                if tx or ty:
                    remote(
                        mine, mine, t_send.at[r - 1], t_recv.at[r - 1],
                        (lax.rem(me_x + halves * tx, nx), lax.rem(me_y + ty, ny)),
                    ).start()

    def all_terms(r, rows):
        every = terms.at[r].reshape(nx * ny, 16, nc).at[pl.ds(0, others), pl.ds(0, rows)]
        return remote(
            every, every, t_send.at[r - 1], t_recv.at[r - 1], (me_x, lax.rem(me_y + 1, ny))
        )

    def pair_terms(r, rows):
        mine = terms.at[r, :, side, :, pl.ds(0, rows)]
        return remote(
            mine, mine, x_send.at[r - 1], x_recv.at[r - 1], (me_x + 1 - 2 * side, me_y)
        )

    def terms_arrived(r, rows):
        all_terms(r, rows).wait_recv()
        if halves == 2:
            pair_terms(r, rows).start()
            pair_terms(r, rows).wait_recv()

    def totals(r, rows):
        return jnp.sum(terms[r, :, :, :, 0:rows, :].reshape(nx * ny, rows, nc), axis=0)

    solve(0)
    gather_alpha()
    for f in range(2):
        mult_ref[face(f), :] = mode_image(f)

    l_copy.wait()
    for f in range(2):
        @pl.when(exists[2 + f])
        def _():
            loads_copy(f).wait_recv()
    for f in range(4):
        values = loads4[face(f), :]
        if f >= 2:
            high, mid, low = split3(values)
            both = dot32(swap[f], beside(high, mid))
            values = both[:, 0:nc] + (both[:, nc : 2 * nc] + dot32(swap[f], low))
        loads4[face(f), :] = values * free4[face(f), :]

    lanes = lax.broadcasted_iota(jnp.int32, (h, nc), 1)
    for f in (EAST, WEST, SOUTH, NORTH):
        @pl.when(exists[f])
        def _():
            g = OPPOSITE[f]
            remote(
                fold_out.at[g], fold_in.at[f], fold_send.at[g], fold_recv.at[f], place[f]
            ).wait_recv()

        came = fold_in[f]
        parts = []
        for b in range(PIECES):
            moved = came if b == 0 else pltpu.roll(came, nc - b * lane_step, 1)
            parts.append(jnp.where(lanes < lane_step, moved, 0.0))
        far = exchanged(f, rows_of(*parts))
        values = (fp_f[face(f), :] + pltpu.roll(far, lane_step, 1)) * free4[face(f), :]
        high, low = split(values)
        images[f, pl.ds(0, lf), :] = (
            high.astype(F32) + pltpu.roll(low.astype(F32), half, 1)
        ).astype(BF16)

    def put_field(f, values):
        high, low = split(values)
        vsplit[face(f), 0:nc] = high
        vsplit[face(f), nc : 2 * nc] = low

    for f in range(4):
        v = dual_mode_image(f) - loads4[face(f), :]
        put_field(f, v)
        if f < 2:
            p_f[face(f), :] = v

    coarse_terms(1)
    spread_terms(1, 8)
    apply_start(1)
    terms_arrived(1, 8)
    solve(1)
    gather_alpha()

    def applied(r, f):
        return free4[face(f), :] * (outbox[r - 1, f] + exchanged(f, inbox[r - 1, f]))

    for f in range(4):
        fp_f[face(f), :] = dual_mode_image(f)
    for f in range(2):
        p = p_f[face(f), :] - mode_image(f)
        p_f[face(f), :] = p
        d_f[face(f), :] = p
    for f in (SOUTH, NORTH, EAST, WEST):
        face_arrived(1, f)
        q = applied(1, f) - fp_f[face(f), :]
        q_f[face(f), :] = q
        fp_f[face(f), :] = q
        put_field(f, q)

    norm = None
    for step in range(ITERS):
        r = step + 2
        last = step + 1 == ITERS
        rows = 8 if last else 9
        coarse_terms(r)
        terms[r, me_h, side, me_y, 6:7, :] = own_sum(d_f, q_f)
        if not last:
            terms[r, me_h, side, me_y, 7:8, :] = own_sum(p_f, p_f if step == 0 else q_f)
            terms[r, me_h, side, me_y, 8:9, :] = own_sum(q_f, q_f)
        spread_terms(r, rows)
        if not last:
            apply_start(r)
        terms_arrived(r, rows)
        inner = solve(r)
        gather_alpha()
        total = totals(r, rows)
        curvature = total[6:7, :]
        if step == 0:
            norm = total[7:8, :]
            cross = curvature
        else:
            cross = total[7:8, :]
        size = norm / curvature
        if last:
            mult_ref[...] = mult_ref[...] + size * d_f[...]
            for f in range(2):
                proj_ref[face(f), :] = p_f[face(f), :] + size * (q_f[face(f), :] - mode_image(f))
            break
        norm_next = norm + 2.0 * size * cross + size * size * (total[8:9, :] - inner)
        ratio = norm_next / norm
        for f in range(4):
            fp_f[face(f), :] = fp_f[face(f), :] - size * dual_mode_image(f)
        for f in range(2):
            d = d_f[face(f), :]
            p = p_f[face(f), :] + size * (q_f[face(f), :] - mode_image(f))
            mult_ref[face(f), :] = mult_ref[face(f), :] + size * d
            p_f[face(f), :] = p
            d_f[face(f), :] = p + ratio * d
        for f in (SOUTH, NORTH, EAST, WEST):
            face_arrived(r, f)
            fp = fp_f[face(f), :] + size * applied(r, f)
            fp_f[face(f), :] = fp
            q = fp + ratio * q_f[face(f), :]
            q_f[face(f), :] = q
            put_field(f, q)
        norm = norm_next

    for r in range(1, ROUNDS):
        rows = 8 if r in (1, ROUNDS - 1) else 9
        all_terms(r, rows).wait_send()
        if halves == 2:
            pair_terms(r, rows).wait_send()
    for stage in coarse_stages:
        column_all(stage).wait_send()
        row_all(stage).wait_send()
    for f in range(2):
        @pl.when(exists[f])
        def _():
            to_owned(f).wait_send()
            loads_copy(f).wait_send()

        @pl.when(exists[2 + f])
        def _():
            to_owner(f).wait_send()
    for f in range(4):
        @pl.when(exists[f])
        def _():
            fold_copy(f).wait_send()
            remote(
                outbox.at[:, f], inbox.at[:, f], face_send.at[f], face_recv.at[0, f], place[f]
            ).wait_send()


def solution(mesh):
    nx, ny = mesh.shape["gx"], mesh.shape["gy"]

    def local(dual_ops, loads, coarse_rhs, coarse_modes, free_mask, face_match, coarse_rows):
        lm = dual_ops.shape[-1]
        lf, nc = loads.shape[-2:]
        wide = nx * ny * 8
        halves = 2 if nx % 2 == 0 else 1
        vmem = pl.BlockSpec(memory_space=pltpu.VMEM)
        hbm = pl.BlockSpec(memory_space=pl.ANY)
        dma = pltpu.SemaphoreType.DMA
        out = jax.ShapeDtypeStruct((2 * lf, nc), F32)
        field = pltpu.VMEM((lm, nc), F32)
        own = pltpu.VMEM((2 * lf, nc), F32)
        mult, proj = pl.pallas_call(
            functools.partial(kernel, nx, ny),
            out_shape=(pltpu.VMEM((2 * lf, nc), F32),) * 2,
            in_specs=[hbm, hbm] + [vmem] * 5,
            out_specs=(vmem, vmem),
            scratch_shapes=[
                pltpu.VMEM((lm, lm), F32),
                pltpu.VMEM((lm, lm), BF16),
                pltpu.VMEM((lm, lm), BF16),
                field,
                pltpu.VMEM((2, 24, lf), F32),
                pltpu.VMEM((2, 24, lf), F32),
                pltpu.VMEM((2, 8, lf), F32),
                pltpu.VMEM((2, 8, lf), F32),
                pltpu.VMEM((nx, ny, 8, wide), F32),
                pltpu.VMEM((wide, 4 * wide), BF16),
                pltpu.VMEM((ROUNDS, nx // halves, halves, ny, 16, nc), F32),
                pltpu.VMEM((nx * ny, 8, nc), F32),
                pltpu.VMEM((4, nc // 2, nc), F32),
                pltpu.VMEM((16, lm), F32),
                pltpu.VMEM((16, lm), BF16),
                pltpu.VMEM((4, 2 * lf, nc), BF16),
                field,
                pltpu.VMEM((nc, lf), F32),
                pltpu.VMEM((4, lf, lf), BF16),
                pltpu.VMEM((lm, 2 * nc), BF16),
                pltpu.VMEM((4, lf // PIECES, nc), F32),
                pltpu.VMEM((4, lf // PIECES, nc), F32),
                pltpu.VMEM((APPLIES - 1, 4, lf, nc), F32),
                pltpu.VMEM((APPLIES - 1, 4, lf, nc), F32),
                own, own, field, field,
                dma((2 * PIECES,)),
                dma,
                dma((4,)),
                dma((APPLIES - 1, 4)),
                dma((4,)), dma((4,)),
                dma((2,)), dma((2,)), dma((2,)), dma((2,)), dma((2,)), dma((2,)),
                dma, dma, dma, dma, dma, dma, dma, dma,
                dma((ROUNDS - 1,)), dma((ROUNDS - 1,)), dma((ROUNDS - 1,)), dma((ROUNDS - 1,)),
            ],
            compiler_params=pltpu.CompilerParams(
                collective_id=0, has_side_effects=True, vmem_limit_bytes=60 * 1024 * 1024
            ),
        )(
            dual_ops.reshape(lm, lm),
            loads.reshape(2 * lf, nc),
            coarse_rhs.reshape(coarse_rhs.shape[2], 1, nc),
            jnp.swapaxes(coarse_modes.reshape(coarse_modes.shape[2:]), 1, 2),
            free_mask.reshape(free_mask.shape[2:]),
            face_match.reshape(face_match.shape[2:]),
            coarse_rows.reshape(-1, 1, coarse_rows.shape[-1]),
        )
        return (mult.reshape(1, 1, 2, lf, nc), proj.reshape(1, 1, 2, lf, nc))

    in_specs = (
        P("gx", "gy", None, None),
        P("gx", "gy", None, None, None),
        P("gx", "gy", None, None),
        P("gx", "gy", None, None, None, None),
        P("gx", "gy", None, None),
        P("gx", "gy", None, None),
        P("gx", "gy", None, None, None),
    )
    out_specs = (P("gx", "gy", None, None, None), P("gx", "gy", None, None, None))
    return jax.shard_map(local, mesh=mesh, in_specs=in_specs, out_specs=out_specs, check_vma=False)
```

```python
import functools

import jax
import jax.numpy as jnp
from jax import lax
from jax.experimental import pallas as pl
from jax.experimental.pallas import tpu as pltpu
from jax.sharding import PartitionSpec as P

ITERS = 3
F32 = jnp.float32
BF16 = jnp.bfloat16
MESH = pl.DeviceIdType.MESH
EAST, SOUTH, WEST, NORTH = 0, 1, 2, 3
OPPOSITE = (WEST, NORTH, EAST, SOUTH)
ROUNDS = ITERS + 2
APPLIES = ITERS + 1
PIECES = 4
ROW_AFTER = 1
CELLS = (
    ((WEST, 0), (EAST, 0)),
    ((WEST, 1), (EAST, 1), (NORTH, 0), (SOUTH, 0)),
    ((WEST, 2), (EAST, 2), (NORTH, 1), (SOUTH, 1)),
    ((WEST, 3), (EAST, 3), (NORTH, 2), (SOUTH, 2)),
    ((NORTH, 3), (SOUTH, 3)),
)
ORDER = tuple(cell for cells in CELLS for cell in cells)
AROUND = ((0, 0), (0, 1), (1, 0), (0, -1), (-1, 0))


def split(values):
    high = values.astype(BF16)
    low = (values - high.astype(F32)).astype(BF16)
    return high, low


def split3(values):
    high = values.astype(BF16)
    rest = values - high.astype(F32)
    mid, low = split(rest)
    return high, mid, low


def dot32(left, right):
    return jnp.dot(left, right, preferred_element_type=F32)


def rows_of(*parts):
    return jnp.concatenate(parts, axis=0)


def beside(*parts):
    return jnp.concatenate(parts, axis=1)


def kernel(
    nx, ny, a_hbm, loads_hbm, rhs_ref, modes_ref, free_ref, match_ref, rows_ref,
    mult_ref, proj_ref,
    a_stage, a_high, a_low, loads4, pack, nb_pack, mpack, nb_match, inverse, inv_parts, terms, alphas,
    alpha_cat, gt8, gtb, images, free4, put, swap, vsplit, fold_out, fold_in, outbox, inbox,
    p_f, d_f, q_f, fp_f,
    a_sem, l_sem, face_send, face_recv, fold_send, fold_recv, pk_send, pk_recv, mp_send, mp_recv,
    ld_send, ld_recv, gy_send, gy_recv, gx_send, gx_recv, cy_send, cy_recv, cx_send, cx_recv,
    t_send, t_recv, x_send, x_recv,
):
    lf = free_ref.shape[1]
    nc = mult_ref.shape[1]
    lm = a_high.shape[0]
    modes = rhs_ref.shape[0]
    ncoarse = rows_ref.shape[2]
    wide = inverse.shape[3]
    halves = terms.shape[2]
    h = lf // PIECES
    lane_step = nc // PIECES
    half = nc // 2
    me_x = lax.axis_index("gx")
    me_y = lax.axis_index("gy")
    me_h, side = me_x // halves, lax.rem(me_x, halves)
    exists = (me_y < ny - 1, me_x < nx - 1, me_y > 0, me_x > 0)
    place = ((me_x, me_y + 1), (me_x + 1, me_y), (me_x, me_y - 1), (me_x - 1, me_y))

    def face(f):
        return pl.ds(f * lf, lf)

    def piece(f, b):
        return pl.ds(f * lf + b * h, h)

    chunks = 2 * PIECES
    chunk = lm // chunks
    a_copies = [
        pltpu.make_async_copy(
            a_hbm.at[pl.ds(i * chunk, chunk)], a_stage.at[pl.ds(i * chunk, chunk)], a_sem.at[i]
        )
        for i in range(chunks)
    ]
    for copy in a_copies:
        copy.start()
    l_copy = pltpu.make_async_copy(loads_hbm, loads4.at[pl.ds(0, 2 * lf)], l_sem)
    l_copy.start()

    unsent = 8 - modes
    inverse[:, :, modes:8, :] = jnp.zeros((nx, ny, unsent, wide), F32)
    for r in (0, 1, ROUNDS - 1):
        terms[r, :, :, :, modes:8, :] = jnp.zeros(terms.shape[1:4] + (unsent, nc), F32)

    barrier = pltpu.get_barrier_semaphore()
    for t in range(1, nx):
        pl.semaphore_signal(
            barrier, inc=1, device_id=(lax.rem(me_x + t, nx), me_y), device_id_type=MESH
        )
    for t in range(1, ny):
        pl.semaphore_signal(
            barrier, inc=1, device_id=(me_x, lax.rem(me_y + t, ny)), device_id_type=MESH
        )

    pack[...] = jnp.zeros_like(pack)
    mpack[...] = jnp.zeros_like(mpack)
    for f in range(2):
        pack[f, 0:modes, :] = modes_ref[f, :, 0, :]
        pack[f, 8 : 8 + modes, :] = modes_ref[f, :, 1, :]
        pack[f, 16:17, :] = free_ref[f : f + 1, :].astype(F32)
        mpack[f, 0:1, :] = match_ref[f : f + 1, :].astype(F32)

    row = lax.broadcasted_iota(jnp.int32, (ncoarse, wide), 0)
    col = lax.broadcasted_iota(jnp.int32, (ncoarse, wide), 1)
    slot = jnp.bitwise_and(col, 7)
    spread = jnp.where((row == modes * jnp.right_shift(col, 3) + slot) & (slot < modes), 1.0, 0.0)
    inverse[me_x, me_y, 0:modes, :] = jnp.dot(
        rows_ref[0:modes, 0, :], spread.astype(F32), precision=lax.Precision.HIGHEST,
        preferred_element_type=F32,
    )
    terms[0, me_h, side, me_y, 0:modes, :] = rhs_ref[:, 0, :]

    pl.semaphore_wait(barrier, nx + ny - 2)

    def remote(src, dst, send, recv, where):
        return pltpu.make_async_remote_copy(
            src_ref=src, dst_ref=dst, send_sem=send, recv_sem=recv,
            device_id=where, device_id_type=MESH,
        )

    def to_owned(f):
        return remote(pack.at[f], nb_pack.at[f], pk_send.at[f], pk_recv.at[f], place[f])

    def to_owner(f):
        return remote(mpack.at[f], nb_match.at[f], mp_send.at[f], mp_recv.at[f], place[2 + f])

    def loads_copy(f):
        return remote(
            loads_hbm.at[face(f)], loads4.at[face(2 + f)], ld_send.at[f], ld_recv.at[f], place[f]
        )

    for f in range(2):
        @pl.when(exists[f])
        def _():
            to_owned(f).start()

        @pl.when(exists[2 + f])
        def _():
            to_owner(f).start()

    own_rows = pl.ds(0, modes)
    coarse_stages = (
        (
            lambda n: inverse.at[me_x, pl.ds(0, n), own_rows], inverse.at[me_x, me_y, own_rows], cy_send, cy_recv,
            lambda n: inverse.at[pl.ds(0, n), :, own_rows], inverse.at[me_x, :, own_rows], cx_send, cx_recv,
        ),
        (
            lambda n: terms.at[0, 0, 0, pl.ds(0, n), own_rows],
            terms.at[0, me_h, side, me_y, own_rows], gy_send, gy_recv,
            lambda n: terms.at[0].reshape(nx, ny, 16, nc).at[pl.ds(0, n), :, own_rows],
            terms.at[0, me_h, side, :, own_rows], gx_send, gx_recv,
        ),
    )

    def column_begin():
        for _, mine, send, recv, _, _, _, _ in coarse_stages:
            for t in range(1, ny):
                remote(mine, mine, send, recv, (me_x, lax.rem(me_y + t, ny))).start()

    def column_all(stage):
        view, _, send, recv, _, _, _, _ = stage
        return remote(view(ny - 1), view(ny - 1), send, recv, (me_x, lax.rem(me_y + 1, ny)))

    def row_begin():
        for stage in coarse_stages:
            column_all(stage).wait_recv()
        for _, _, _, _, _, mine, send, recv in coarse_stages:
            for t in range(1, nx):
                remote(mine, mine, send, recv, (lax.rem(me_x + t, nx), me_y)).start()

    def row_all(stage):
        _, _, _, _, view, _, send, recv = stage
        return remote(view(nx - 1), view(nx - 1), send, recv, (lax.rem(me_x + 1, nx), me_y))

    column_begin()
    for f in range(2):
        @pl.when(exists[f])
        def _():
            loads_copy(f).start()

    for f in range(4):
        @pl.when(jnp.logical_not(exists[f]))
        def _():
            fold_in[f] = jnp.zeros((h, nc), F32)
            for r in range(1, APPLIES):
                inbox[r - 1, f] = jnp.zeros((lf, nc), F32)
    for f in range(2):
        @pl.when(jnp.logical_not(exists[f]))
        def _():
            nb_match[f] = jnp.zeros((8, lf), F32)

        @pl.when(jnp.logical_not(exists[2 + f]))
        def _():
            nb_pack[f] = jnp.zeros((24, lf), F32)
            loads4[face(2 + f), :] = jnp.zeros((lf, nc), F32)

    def cast_chunk(i):
        a_copies[i].wait()
        for t in range(2):
            f, b = divmod(2 * i + t, PIECES)
            high, low = split(a_stage[piece(f, b), :])
            to = pl.ds(ORDER.index((f, b)) * h, h)
            a_high[to, :] = high
            a_low[to, :] = low

    for i in range(chunks):
        cast_chunk(i)

    slots = lax.broadcasted_iota(jnp.int32, (lf, lf), 0)
    backs = []
    for f in range(2):
        back = jnp.where(slots == match_ref[f : f + 1, :], 1.0, 0.0).astype(F32)
        swap[2 + f] = (-jnp.transpose(back)).astype(BF16)
        backs.append(back.astype(BF16))

    def prepare(f):
        if f < 2:
            mask = pack[f, 16:17, :]
            owner = pack[f, 0:8, :] * mask
            other = pack[f, 8:16, :] * mask
            own_part, far_part = owner, other
        else:
            high, low = split(nb_pack[f - 2])
            local = dot32(high, backs[f - 2]) + dot32(low, backs[f - 2])
            mask = local[16:17, :]
            own_part = -local[8:16, :] * mask
            far_part = -local[0:8, :] * mask
        put[...] = jnp.zeros_like(put)
        put[0:modes, :] = own_part[0:modes, :]
        put[modes * (f + 1) : modes * (f + 2), :] = far_part[0:modes, :]
        high, low = split(own_part)
        gt8[0:8, face(f)] = high.astype(F32)
        gt8[8:16, face(f)] = low.astype(F32)
        high, low = split(jnp.transpose(put[...]))
        vsplit[face(f), 0:nc] = high
        vsplit[face(f), nc : 2 * nc] = low
        if f < 2:
            images[f, pl.ds(lf, lf), :] = (
                high.astype(F32) + pltpu.roll(low.astype(F32), half, 1)
            ).astype(BF16)
        free4[face(f), :] = jnp.transpose(jnp.broadcast_to(mask, (nc, lf)))

    near, far_half = pl.ds(0, 2 * lf), pl.ds(2 * lf, 2 * lf)

    def block_half(cells, part):
        at = pl.ds(ORDER.index(cells[0]) * h, len(cells) * h)
        both = dot32(a_high[at, part], vsplit[part, :])
        z = dot32(a_low[at, part], vsplit[part, 0:nc])
        return z + both[:, 0:nc] + both[:, nc : 2 * nc]

    for f in range(2):
        prepare(f)
    for cells in CELLS:
        z = block_half(cells, near)
        for i, (f, b) in enumerate(cells):
            fp_f[piece(f, b), :] = z[i * h : (i + 1) * h, :]

    row_begin()
    for f in range(2):
        @pl.when(exists[2 + f])
        def _():
            to_owned(f).wait_recv()

    for f in range(2, 4):
        prepare(f)
    gtb[...] = gt8[...].astype(BF16)

    def face_copy(r, f, b):
        g = OPPOSITE[f]
        part = pl.ds(b * h, h)
        return remote(
            outbox.at[r - 1, f, part], inbox.at[r - 1, g, part],
            face_send.at[f], face_recv.at[r - 1, g], place[f],
        )

    def block(cells):
        at = pl.ds(ORDER.index(cells[0]) * h, len(cells) * h)
        both = dot32(a_high[at, :], vsplit[...])
        z = dot32(a_low[at, :], vsplit[:, 0:nc])
        return z + both[:, 0:nc] + both[:, nc : 2 * nc]

    def apply_start(r):
        for cells in CELLS:
            z = block(cells)
            for i, (f, b) in enumerate(cells):
                outbox[r - 1, f, pl.ds(b * h, h), :] = z[i * h : (i + 1) * h, :]
            for f, b in cells:
                @pl.when(exists[f])
                def _():
                    face_copy(r, f, b).start()

    def face_arrived(r, f):
        g = OPPOSITE[f]

        @pl.when(exists[f])
        def _():
            remote(
                outbox.at[r - 1, g], inbox.at[r - 1, f], face_send.at[g], face_recv.at[r - 1, f],
                place[f],
            ).wait_recv()

    def exchanged(f, values):
        high, low = split(values)
        both = dot32(swap[f], beside(high, low))
        return both[:, 0:nc] + both[:, nc : 2 * nc]

    def fold_copy(f):
        g = OPPOSITE[f]
        return remote(
            fold_out.at[f], fold_in.at[g], fold_send.at[f], fold_recv.at[g], place[f]
        )

    for cells in CELLS:
        z = block_half(cells, far_half)
        for i, (f, b) in enumerate(cells):
            part = fp_f[piece(f, b), :] + z[i * h : (i + 1) * h, :]
            fp_f[piece(f, b), :] = part
            if b == 0:
                fold_out[f] = part
            else:
                fold_out[f] = fold_out[f] + pltpu.roll(part, b * lane_step, 1)
    for f in (WEST, EAST, NORTH, SOUTH):
        @pl.when(exists[f])
        def _():
            fold_copy(f).start()

    for f in range(2):
        @pl.when(exists[f])
        def _():
            remote(
                mpack.at[f], nb_match.at[f], mp_send.at[f], mp_recv.at[f], place[f]
            ).wait_recv()

        back = jnp.where(slots == nb_match[f, 0:1, :].astype(jnp.int32), -1.0, 0.0)
        swap[f] = back.astype(BF16)

    alpha_cat[...] = jnp.zeros_like(alpha_cat)
    for stage in coarse_stages:
        row_all(stage).wait_recv()
    high, mid, low = split3(inverse[...].reshape(nx * ny * 8, wide))
    inv_parts[:, 0:wide] = high
    inv_parts[:, wide : 2 * wide] = mid
    inv_parts[:, 2 * wide : 3 * wide] = low
    inv_parts[:, 3 * wide : 4 * wide] = high

    def coarse_terms(r):
        both = dot32(gtb[...], vsplit[...])
        terms[r, me_h, side, me_y, 0:8, :] = (
            both[0:8, 0:nc] + both[0:8, nc : 2 * nc] + both[8:16, 0:nc]
        )

    def solve(r):
        c = terms[r, :, :, :, 0:8, :].reshape(nx * ny * 8, nc)
        high, mid, low = split3(c)
        nothing = jnp.zeros_like(high)
        right = rows_of(
            beside(high, mid), beside(high, mid), beside(high, nothing), beside(low, nothing)
        )
        both = dot32(inv_parts[...], right)
        alpha = both[:, 0:nc] + both[:, nc : 2 * nc]
        alphas[...] = alpha.reshape(nx * ny, 8, nc)
        return jnp.sum(c * alpha, axis=0, keepdims=True)

    def gather_alpha():
        for which in range(5):
            x, y = (me_x, me_y) if which == 0 else place[which - 1]
            for k, (dx, dy) in enumerate(AROUND):
                xx = jnp.clip(x + dx, 0, nx - 1)
                yy = jnp.clip(y + dy, 0, ny - 1)
                values = alphas[xx * ny + yy][0:modes, :]
                if which == 0:
                    for f in range(4):
                        alpha_cat[f, modes * k : modes * (k + 1), :] = values
                else:
                    alpha_cat[
                        which - 1, lane_step + modes * k : lane_step + modes * (k + 1), :
                    ] = values

    def right_side(f):
        high, low = split(alpha_cat[f])
        return rows_of(beside(high, low), beside(high, jnp.zeros_like(high)))

    def dual_mode_image(f):
        both = dot32(images[f, pl.ds(0, lf), :], right_side(f))
        return both[:, 0:nc] + both[:, nc : 2 * nc]

    def mode_image(f):
        both = dot32(images[f, pl.ds(lf, lf), :], right_side(f))
        return both[:, 0:nc] + both[:, nc : 2 * nc]

    def own_sum(left, right):
        return jnp.sum(
            left[0 : 2 * lf, :] * right[0 : 2 * lf, :], axis=0, keepdims=True
        )

    def rows_in(r):
        return modes if r == 1 else modes + 1 if r == ROUNDS - 1 else modes + 3

    def stride(r):
        return 1 if r == ROUNDS - 1 else halves

    def spread_terms(r, rows):
        mine = terms.at[r, me_h, side, me_y, pl.ds(0, rows)]
        for tx in range(nx // stride(r)):
            for ty in range(ny):
                if tx or ty:
                    remote(
                        mine, mine, t_send.at[r - 1], t_recv.at[r - 1],
                        (lax.rem(me_x + stride(r) * tx, nx), lax.rem(me_y + ty, ny)),
                    ).start()

    def all_terms(r, rows):
        others = nx * ny // stride(r) - 1
        every = terms.at[r].reshape(nx * ny, 16, nc).at[pl.ds(0, others), pl.ds(0, rows)]
        return remote(
            every, every, t_send.at[r - 1], t_recv.at[r - 1], (me_x, lax.rem(me_y + 1, ny))
        )

    def pair_terms(r, rows):
        mine = terms.at[r, :, side, :, pl.ds(0, rows)]
        return remote(
            mine, mine, x_send.at[r - 1], x_recv.at[r - 1], (me_x + 1 - 2 * side, me_y)
        )

    def terms_arrived(r, rows):
        all_terms(r, rows).wait_recv()
        if stride(r) == 2:
            pair_terms(r, rows).start()
            pair_terms(r, rows).wait_recv()

    def totals(r):
        return jnp.sum(terms[r, :, :, :, 0:16, :].reshape(nx * ny, 16, nc), axis=0)

    solve(0)
    gather_alpha()
    for f in range(2):
        mult_ref[face(f), :] = mode_image(f)

    l_copy.wait()
    for f in range(2):
        @pl.when(exists[2 + f])
        def _():
            loads_copy(f).wait_recv()
    for f in range(4):
        values = loads4[face(f), :]
        if f >= 2:
            high, mid, low = split3(values)
            both = dot32(swap[f], beside(high, mid))
            values = both[:, 0:nc] + (both[:, nc : 2 * nc] + dot32(swap[f], low))
        loads4[face(f), :] = values * free4[face(f), :]

    lanes = lax.broadcasted_iota(jnp.int32, (h, nc), 1)
    for f in (EAST, WEST, SOUTH, NORTH):
        @pl.when(exists[f])
        def _():
            g = OPPOSITE[f]
            remote(
                fold_out.at[g], fold_in.at[f], fold_send.at[g], fold_recv.at[f], place[f]
            ).wait_recv()

        came = fold_in[f]
        parts = []
        for b in range(PIECES):
            moved = came if b == 0 else pltpu.roll(came, nc - b * lane_step, 1)
            parts.append(jnp.where(lanes < lane_step, moved, 0.0))
        far = exchanged(f, rows_of(*parts))
        values = (fp_f[face(f), :] + pltpu.roll(far, lane_step, 1)) * free4[face(f), :]
        high, low = split(values)
        images[f, pl.ds(0, lf), :] = (
            high.astype(F32) + pltpu.roll(low.astype(F32), half, 1)
        ).astype(BF16)

    def put_field(f, values):
        high, low = split(values)
        vsplit[face(f), 0:nc] = high
        vsplit[face(f), nc : 2 * nc] = low

    for f in range(4):
        v = dual_mode_image(f) - loads4[face(f), :]
        put_field(f, v)
        if f < 2:
            p_f[face(f), :] = v

    coarse_terms(1)
    spread_terms(1, rows_in(1))
    apply_start(1)
    terms_arrived(1, rows_in(1))
    solve(1)
    gather_alpha()

    def applied(r, f):
        return free4[face(f), :] * (outbox[r - 1, f] + exchanged(f, inbox[r - 1, f]))

    for f in range(4):
        fp_f[face(f), :] = dual_mode_image(f)
    for f in range(2):
        p = p_f[face(f), :] - mode_image(f)
        p_f[face(f), :] = p
        d_f[face(f), :] = p
    for f in (SOUTH, NORTH, EAST, WEST):
        face_arrived(1, f)
        q = applied(1, f) - fp_f[face(f), :]
        q_f[face(f), :] = q
        fp_f[face(f), :] = q
        put_field(f, q)

    norm = None
    for step in range(ITERS):
        r = step + 2
        last = step + 1 == ITERS
        rows = rows_in(r)
        coarse_terms(r)
        terms[r, me_h, side, me_y, modes : modes + 1, :] = own_sum(d_f, q_f)
        if not last:
            terms[r, me_h, side, me_y, modes + 1 : modes + 2, :] = own_sum(
                p_f, p_f if step == 0 else q_f
            )
            terms[r, me_h, side, me_y, modes + 2 : modes + 3, :] = own_sum(q_f, q_f)
        spread_terms(r, rows)
        if not last:
            apply_start(r)
        terms_arrived(r, rows)
        inner = solve(r)
        gather_alpha()
        total = totals(r)
        curvature = total[6:7, :]
        if step == 0:
            norm = total[7:8, :]
            cross = curvature
        else:
            cross = total[7:8, :]
        size = norm / curvature
        if last:
            mult_ref[...] = mult_ref[...] + size * d_f[...]
            for f in range(2):
                proj_ref[face(f), :] = p_f[face(f), :] + size * (q_f[face(f), :] - mode_image(f))
            break
        norm_next = norm + 2.0 * size * cross + size * size * (total[8:9, :] - inner)
        ratio = norm_next / norm
        for f in range(4):
            fp_f[face(f), :] = fp_f[face(f), :] - size * dual_mode_image(f)
        for f in range(2):
            d = d_f[face(f), :]
            p = p_f[face(f), :] + size * (q_f[face(f), :] - mode_image(f))
            mult_ref[face(f), :] = mult_ref[face(f), :] + size * d
            p_f[face(f), :] = p
            d_f[face(f), :] = p + ratio * d
        for f in (SOUTH, NORTH, EAST, WEST):
            face_arrived(r, f)
            fp = fp_f[face(f), :] + size * applied(r, f)
            fp_f[face(f), :] = fp
            q = fp + ratio * q_f[face(f), :]
            q_f[face(f), :] = q
            put_field(f, q)
        norm = norm_next

    for r in range(1, ROUNDS):
        rows = rows_in(r)
        all_terms(r, rows).wait_send()
        if stride(r) == 2:
            pair_terms(r, rows).wait_send()
    for stage in coarse_stages:
        column_all(stage).wait_send()
        row_all(stage).wait_send()
    for f in range(2):
        @pl.when(exists[f])
        def _():
            to_owned(f).wait_send()
            loads_copy(f).wait_send()

        @pl.when(exists[2 + f])
        def _():
            to_owner(f).wait_send()
    for f in range(4):
        @pl.when(exists[f])
        def _():
            fold_copy(f).wait_send()
            remote(
                outbox.at[:, f], inbox.at[:, f], face_send.at[f], face_recv.at[0, f], place[f]
            ).wait_send()


def solution(mesh):
    nx, ny = mesh.shape["gx"], mesh.shape["gy"]

    def local(dual_ops, loads, coarse_rhs, coarse_modes, free_mask, face_match, coarse_rows):
        lm = dual_ops.shape[-1]
        lf, nc = loads.shape[-2:]
        wide = nx * ny * 8
        halves = 2 if nx % 2 == 0 else 1
        vmem = pl.BlockSpec(memory_space=pltpu.VMEM)
        hbm = pl.BlockSpec(memory_space=pl.ANY)
        dma = pltpu.SemaphoreType.DMA
        out = jax.ShapeDtypeStruct((2 * lf, nc), F32)
        field = pltpu.VMEM((lm, nc), F32)
        own = pltpu.VMEM((2 * lf, nc), F32)
        mult, proj = pl.pallas_call(
            functools.partial(kernel, nx, ny),
            out_shape=(pltpu.VMEM((2 * lf, nc), F32),) * 2,
            in_specs=[hbm, hbm] + [vmem] * 5,
            out_specs=(vmem, vmem),
            scratch_shapes=[
                pltpu.VMEM((lm, lm), F32),
                pltpu.VMEM((lm, lm), BF16),
                pltpu.VMEM((lm, lm), BF16),
                field,
                pltpu.VMEM((2, 24, lf), F32),
                pltpu.VMEM((2, 24, lf), F32),
                pltpu.VMEM((2, 8, lf), F32),
                pltpu.VMEM((2, 8, lf), F32),
                pltpu.VMEM((nx, ny, 8, wide), F32),
                pltpu.VMEM((wide, 4 * wide), BF16),
                pltpu.VMEM((ROUNDS, nx // halves, halves, ny, 16, nc), F32),
                pltpu.VMEM((nx * ny, 8, nc), F32),
                pltpu.VMEM((4, nc // 2, nc), F32),
                pltpu.VMEM((16, lm), F32),
                pltpu.VMEM((16, lm), BF16),
                pltpu.VMEM((4, 2 * lf, nc), BF16),
                field,
                pltpu.VMEM((nc, lf), F32),
                pltpu.VMEM((4, lf, lf), BF16),
                pltpu.VMEM((lm, 2 * nc), BF16),
                pltpu.VMEM((4, lf // PIECES, nc), F32),
                pltpu.VMEM((4, lf // PIECES, nc), F32),
                pltpu.VMEM((APPLIES - 1, 4, lf, nc), F32),
                pltpu.VMEM((APPLIES - 1, 4, lf, nc), F32),
                own, own, field, field,
                dma((2 * PIECES,)),
                dma,
                dma((4,)),
                dma((APPLIES - 1, 4)),
                dma((4,)), dma((4,)),
                dma((2,)), dma((2,)), dma((2,)), dma((2,)), dma((2,)), dma((2,)),
                dma, dma, dma, dma, dma, dma, dma, dma,
                dma((ROUNDS - 1,)), dma((ROUNDS - 1,)), dma((ROUNDS - 1,)), dma((ROUNDS - 1,)),
            ],
            compiler_params=pltpu.CompilerParams(
                collective_id=0, has_side_effects=True, vmem_limit_bytes=60 * 1024 * 1024
            ),
        )(
            dual_ops.reshape(lm, lm),
            loads.reshape(2 * lf, nc),
            coarse_rhs.reshape(coarse_rhs.shape[2], 1, nc),
            jnp.swapaxes(coarse_modes.reshape(coarse_modes.shape[2:]), 1, 2),
            free_mask.reshape(free_mask.shape[2:]),
            face_match.reshape(face_match.shape[2:]),
            coarse_rows.reshape(-1, 1, coarse_rows.shape[-1]),
        )
        return (mult.reshape(1, 1, 2, lf, nc), proj.reshape(1, 1, 2, lf, nc))

    in_specs = (
        P("gx", "gy", None, None),
        P("gx", "gy", None, None, None),
        P("gx", "gy", None, None),
        P("gx", "gy", None, None, None, None),
        P("gx", "gy", None, None),
        P("gx", "gy", None, None),
        P("gx", "gy", None, None, None),
    )
    out_specs = (P("gx", "gy", None, None, None), P("gx", "gy", None, None, None))
    return jax.shard_map(local, mesh=mesh, in_specs=in_specs, out_specs=out_specs, check_vma=False)
```

```python
import functools

import jax
import jax.numpy as jnp
from jax import lax
from jax.experimental import pallas as pl
from jax.experimental.pallas import tpu as pltpu
from jax.sharding import PartitionSpec as P

ITERS = 3
F32 = jnp.float32
BF16 = jnp.bfloat16
MESH = pl.DeviceIdType.MESH
EAST, SOUTH, WEST, NORTH = 0, 1, 2, 3
OPPOSITE = (WEST, NORTH, EAST, SOUTH)
ROUNDS = ITERS + 2
APPLIES = ITERS + 1
PIECES = 4
ROW_AFTER = 1
CELLS = (
    ((WEST, 0), (EAST, 0)),
    ((WEST, 1), (EAST, 1), (NORTH, 0), (SOUTH, 0)),
    ((WEST, 2), (EAST, 2), (NORTH, 1), (SOUTH, 1)),
    ((WEST, 3), (EAST, 3), (NORTH, 2), (SOUTH, 2)),
    ((NORTH, 3), (SOUTH, 3)),
)
ORDER = tuple(cell for cells in CELLS for cell in cells)
AROUND = ((0, 0), (0, 1), (1, 0), (0, -1), (-1, 0))


def split(values):
    high = values.astype(BF16)
    low = (values - high.astype(F32)).astype(BF16)
    return high, low


def split3(values):
    high = values.astype(BF16)
    rest = values - high.astype(F32)
    mid, low = split(rest)
    return high, mid, low


def dot32(left, right):
    return jnp.dot(left, right, preferred_element_type=F32)


def rows_of(*parts):
    return jnp.concatenate(parts, axis=0)


def beside(*parts):
    return jnp.concatenate(parts, axis=1)


def kernel(
    nx, ny, a_hbm, loads_hbm, rhs_ref, modes_ref, free_ref, match_ref, rows_ref,
    mult_ref, proj_ref,
    a_stage, a_high, a_low, loads4, pack, nb_pack, mpack, nb_match, inverse, inv_parts, terms, alphas,
    alpha_cat, gt8, gtb, images, free4, put, swap, vsplit, fold_out, fold_in, outbox, inbox,
    p_f, d_f, q_f, fp_f,
    a_sem, l_sem, face_send, face_recv, fold_send, fold_recv, pk_send, pk_recv, mp_send, mp_recv,
    ld_send, ld_recv, gy_send, gy_recv, gx_send, gx_recv, cy_send, cy_recv, cx_send, cx_recv,
    t_send, t_recv, x_send, x_recv,
):
    lf = free_ref.shape[1]
    nc = mult_ref.shape[1]
    lm = a_high.shape[0]
    modes = rhs_ref.shape[0]
    ncoarse = rows_ref.shape[2]
    wide = inverse.shape[3]
    halves = terms.shape[2]
    h = lf // PIECES
    lane_step = nc // PIECES
    half = nc // 2
    me_x = lax.axis_index("gx")
    me_y = lax.axis_index("gy")
    me_h, side = me_x // halves, lax.rem(me_x, halves)
    exists = (me_y < ny - 1, me_x < nx - 1, me_y > 0, me_x > 0)
    place = ((me_x, me_y + 1), (me_x + 1, me_y), (me_x, me_y - 1), (me_x - 1, me_y))

    def face(f):
        return pl.ds(f * lf, lf)

    def piece(f, b):
        return pl.ds(f * lf + b * h, h)

    chunks = 2 * PIECES
    chunk = lm // chunks
    a_copies = [
        pltpu.make_async_copy(
            a_hbm.at[pl.ds(i * chunk, chunk)], a_stage.at[pl.ds(i * chunk, chunk)], a_sem.at[i]
        )
        for i in range(chunks)
    ]
    for copy in a_copies:
        copy.start()
    l_copy = pltpu.make_async_copy(loads_hbm, loads4.at[pl.ds(0, 2 * lf)], l_sem)
    l_copy.start()

    unsent = 8 - modes
    inverse[:, :, modes:8, :] = jnp.zeros((nx, ny, unsent, wide), F32)
    for r in (0, 1, ROUNDS - 1):
        terms[r, :, :, :, modes:8, :] = jnp.zeros(terms.shape[1:4] + (unsent, nc), F32)

    barrier = pltpu.get_barrier_semaphore()
    for t in range(1, nx):
        pl.semaphore_signal(
            barrier, inc=1, device_id=(lax.rem(me_x + t, nx), me_y), device_id_type=MESH
        )
    for t in range(1, ny):
        pl.semaphore_signal(
            barrier, inc=1, device_id=(me_x, lax.rem(me_y + t, ny)), device_id_type=MESH
        )

    pack[...] = jnp.zeros_like(pack)
    mpack[...] = jnp.zeros_like(mpack)
    for f in range(2):
        pack[f, 0:modes, :] = modes_ref[f, :, 0, :]
        pack[f, 8 : 8 + modes, :] = modes_ref[f, :, 1, :]
        pack[f, 16:17, :] = free_ref[f : f + 1, :].astype(F32)
        mpack[f, 0:1, :] = match_ref[f : f + 1, :].astype(F32)

    row = lax.broadcasted_iota(jnp.int32, (ncoarse, wide), 0)
    col = lax.broadcasted_iota(jnp.int32, (ncoarse, wide), 1)
    slot = jnp.bitwise_and(col, 7)
    spread = jnp.where((row == modes * jnp.right_shift(col, 3) + slot) & (slot < modes), 1.0, 0.0)
    inverse[me_x, me_y, 0:modes, :] = jnp.dot(
        rows_ref[0:modes, 0, :], spread.astype(F32), precision=lax.Precision.HIGHEST,
        preferred_element_type=F32,
    )
    terms[0, me_h, side, me_y, 0:modes, :] = rhs_ref[:, 0, :]

    pl.semaphore_wait(barrier, nx + ny - 2)

    def remote(src, dst, send, recv, where):
        return pltpu.make_async_remote_copy(
            src_ref=src, dst_ref=dst, send_sem=send, recv_sem=recv,
            device_id=where, device_id_type=MESH,
        )

    def to_owned(f):
        return remote(pack.at[f], nb_pack.at[f], pk_send.at[f], pk_recv.at[f], place[f])

    def to_owner(f):
        return remote(mpack.at[f], nb_match.at[f], mp_send.at[f], mp_recv.at[f], place[2 + f])

    def loads_copy(f):
        return remote(
            loads_hbm.at[face(f)], loads4.at[face(2 + f)], ld_send.at[f], ld_recv.at[f], place[f]
        )

    for f in range(2):
        @pl.when(exists[f])
        def _():
            to_owned(f).start()

        @pl.when(exists[2 + f])
        def _():
            to_owner(f).start()

    own_rows = pl.ds(0, modes)
    coarse_stages = (
        (
            lambda n: inverse.at[me_x, pl.ds(0, n), own_rows], inverse.at[me_x, me_y, own_rows], cy_send, cy_recv,
            lambda n: inverse.at[pl.ds(0, n), :, own_rows], inverse.at[me_x, :, own_rows], cx_send, cx_recv,
        ),
        (
            lambda n: terms.at[0, 0, 0, pl.ds(0, n), own_rows],
            terms.at[0, me_h, side, me_y, own_rows], gy_send, gy_recv,
            lambda n: terms.at[0].reshape(nx, ny, 16, nc).at[pl.ds(0, n), :, own_rows],
            terms.at[0, me_h, side, :, own_rows], gx_send, gx_recv,
        ),
    )

    def column_begin():
        for _, mine, send, recv, _, _, _, _ in coarse_stages:
            for t in range(1, ny):
                remote(mine, mine, send, recv, (me_x, lax.rem(me_y + t, ny))).start()

    def column_all(stage):
        view, _, send, recv, _, _, _, _ = stage
        return remote(view(ny - 1), view(ny - 1), send, recv, (me_x, lax.rem(me_y + 1, ny)))

    def row_begin():
        for stage in coarse_stages:
            column_all(stage).wait_recv()
        for _, _, _, _, _, mine, send, recv in coarse_stages:
            for t in range(1, nx):
                remote(mine, mine, send, recv, (lax.rem(me_x + t, nx), me_y)).start()

    def row_all(stage):
        _, _, _, _, view, _, send, recv = stage
        return remote(view(nx - 1), view(nx - 1), send, recv, (lax.rem(me_x + 1, nx), me_y))

    column_begin()
    for f in range(2):
        @pl.when(exists[f])
        def _():
            loads_copy(f).start()

    for f in range(4):
        @pl.when(jnp.logical_not(exists[f]))
        def _():
            fold_in[f] = jnp.zeros((h, nc), F32)
            for r in range(1, APPLIES):
                inbox[r - 1, f] = jnp.zeros((lf, nc), F32)
    for f in range(2):
        @pl.when(jnp.logical_not(exists[f]))
        def _():
            nb_match[f] = jnp.zeros((8, lf), F32)

        @pl.when(jnp.logical_not(exists[2 + f]))
        def _():
            nb_pack[f] = jnp.zeros((24, lf), F32)
            loads4[face(2 + f), :] = jnp.zeros((lf, nc), F32)

    def cast_chunk(i):
        a_copies[i].wait()
        for t in range(2):
            f, b = divmod(2 * i + t, PIECES)
            high, low = split(a_stage[piece(f, b), :])
            to = pl.ds(ORDER.index((f, b)) * h, h)
            a_high[to, :] = high
            a_low[to, :] = low

    for i in range(chunks):
        cast_chunk(i)

    slots = lax.broadcasted_iota(jnp.int32, (lf, lf), 0)
    backs = []
    for f in range(2):
        back = jnp.where(slots == match_ref[f : f + 1, :], 1.0, 0.0).astype(F32)
        swap[2 + f] = (-jnp.transpose(back)).astype(BF16)
        backs.append(back.astype(BF16))

    def prepare(f):
        if f < 2:
            mask = pack[f, 16:17, :]
            owner = pack[f, 0:8, :] * mask
            other = pack[f, 8:16, :] * mask
            own_part, far_part = owner, other
        else:
            high, low = split(nb_pack[f - 2])
            local = dot32(high, backs[f - 2]) + dot32(low, backs[f - 2])
            mask = local[16:17, :]
            own_part = -local[8:16, :] * mask
            far_part = -local[0:8, :] * mask
        put[...] = jnp.zeros_like(put)
        put[0:modes, :] = own_part[0:modes, :]
        put[modes * (f + 1) : modes * (f + 2), :] = far_part[0:modes, :]
        high, low = split(own_part)
        gt8[0:8, face(f)] = high.astype(F32)
        gt8[8:16, face(f)] = low.astype(F32)
        high, low = split(jnp.transpose(put[...]))
        vsplit[face(f), 0:nc] = high
        vsplit[face(f), nc : 2 * nc] = low
        if f < 2:
            images[f, pl.ds(lf, lf), :] = (
                high.astype(F32) + pltpu.roll(low.astype(F32), half, 1)
            ).astype(BF16)
        free4[face(f), :] = jnp.transpose(jnp.broadcast_to(mask, (nc, lf)))

    near, far_half = pl.ds(0, 2 * lf), pl.ds(2 * lf, 2 * lf)

    def block_half(cells, part):
        at = pl.ds(ORDER.index(cells[0]) * h, len(cells) * h)
        both = dot32(a_high[at, part], vsplit[part, :])
        z = dot32(a_low[at, part], vsplit[part, 0:nc])
        return z + both[:, 0:nc] + both[:, nc : 2 * nc]

    for f in range(2):
        prepare(f)
    for cells in CELLS:
        z = block_half(cells, near)
        for i, (f, b) in enumerate(cells):
            fp_f[piece(f, b), :] = z[i * h : (i + 1) * h, :]

    row_begin()
    for f in range(2):
        @pl.when(exists[2 + f])
        def _():
            to_owned(f).wait_recv()

    for f in range(2, 4):
        prepare(f)
    gtb[...] = gt8[...].astype(BF16)

    def face_copy(r, f, b):
        g = OPPOSITE[f]
        part = pl.ds(b * h, h)
        return remote(
            outbox.at[r - 1, f, part], inbox.at[r - 1, g, part],
            face_send.at[f], face_recv.at[r - 1, g], place[f],
        )

    def block(cells):
        at = pl.ds(ORDER.index(cells[0]) * h, len(cells) * h)
        both = dot32(a_high[at, :], vsplit[...])
        z = dot32(a_low[at, :], vsplit[:, 0:nc])
        return z + both[:, 0:nc] + both[:, nc : 2 * nc]

    def apply_start(r):
        for cells in CELLS:
            z = block(cells)
            for i, (f, b) in enumerate(cells):
                outbox[r - 1, f, pl.ds(b * h, h), :] = z[i * h : (i + 1) * h, :]
            for f, b in cells:
                @pl.when(exists[f])
                def _():
                    face_copy(r, f, b).start()

    def face_arrived(r, f):
        g = OPPOSITE[f]

        @pl.when(exists[f])
        def _():
            remote(
                outbox.at[r - 1, g], inbox.at[r - 1, f], face_send.at[g], face_recv.at[r - 1, f],
                place[f],
            ).wait_recv()

    def exchanged(f, values):
        high, low = split(values)
        both = dot32(swap[f], beside(high, low))
        return both[:, 0:nc] + both[:, nc : 2 * nc]

    def applied(r, f):
        return free4[face(f), :] * (outbox[r - 1, f] + exchanged(f, inbox[r - 1, f]))

    def finished(r, f):
        if f in (SOUTH, NORTH):
            return inbox[r - 1, f]
        face_arrived(r, f)
        return applied(r, f)

    def fold_copy(f):
        g = OPPOSITE[f]
        return remote(
            fold_out.at[f], fold_in.at[g], fold_send.at[f], fold_recv.at[g], place[f]
        )

    for cells in CELLS:
        z = block_half(cells, far_half)
        for i, (f, b) in enumerate(cells):
            part = fp_f[piece(f, b), :] + z[i * h : (i + 1) * h, :]
            fp_f[piece(f, b), :] = part
            if b == 0:
                fold_out[f] = part
            else:
                fold_out[f] = fold_out[f] + pltpu.roll(part, b * lane_step, 1)
    for f in (WEST, EAST, NORTH, SOUTH):
        @pl.when(exists[f])
        def _():
            fold_copy(f).start()

    for f in range(2):
        @pl.when(exists[f])
        def _():
            remote(
                mpack.at[f], nb_match.at[f], mp_send.at[f], mp_recv.at[f], place[f]
            ).wait_recv()

        back = jnp.where(slots == nb_match[f, 0:1, :].astype(jnp.int32), -1.0, 0.0)
        swap[f] = back.astype(BF16)

    alpha_cat[...] = jnp.zeros_like(alpha_cat)
    for stage in coarse_stages:
        row_all(stage).wait_recv()
    high, mid, low = split3(inverse[...].reshape(nx * ny * 8, wide))
    inv_parts[:, 0:wide] = high
    inv_parts[:, wide : 2 * wide] = mid
    inv_parts[:, 2 * wide : 3 * wide] = low
    inv_parts[:, 3 * wide : 4 * wide] = high

    def coarse_terms(r):
        both = dot32(gtb[...], vsplit[...])
        terms[r, me_h, side, me_y, 0:8, :] = (
            both[0:8, 0:nc] + both[0:8, nc : 2 * nc] + both[8:16, 0:nc]
        )

    def solve(r):
        c = terms[r, :, :, :, 0:8, :].reshape(nx * ny * 8, nc)
        high, mid, low = split3(c)
        nothing = jnp.zeros_like(high)
        right = rows_of(
            beside(high, mid), beside(high, mid), beside(high, nothing), beside(low, nothing)
        )
        both = dot32(inv_parts[...], right)
        alpha = both[:, 0:nc] + both[:, nc : 2 * nc]
        alphas[...] = alpha.reshape(nx * ny, 8, nc)
        return jnp.sum(c * alpha, axis=0, keepdims=True)

    def gather_alpha():
        for which in range(5):
            x, y = (me_x, me_y) if which == 0 else place[which - 1]
            for k, (dx, dy) in enumerate(AROUND):
                xx = jnp.clip(x + dx, 0, nx - 1)
                yy = jnp.clip(y + dy, 0, ny - 1)
                values = alphas[xx * ny + yy][0:modes, :]
                if which == 0:
                    for f in range(4):
                        alpha_cat[f, modes * k : modes * (k + 1), :] = values
                else:
                    alpha_cat[
                        which - 1, lane_step + modes * k : lane_step + modes * (k + 1), :
                    ] = values

    def right_side(f):
        high, low = split(alpha_cat[f])
        return rows_of(beside(high, low), beside(high, jnp.zeros_like(high)))

    def dual_mode_image(f):
        both = dot32(images[f, pl.ds(0, lf), :], right_side(f))
        return both[:, 0:nc] + both[:, nc : 2 * nc]

    def mode_image(f):
        both = dot32(images[f, pl.ds(lf, lf), :], right_side(f))
        return both[:, 0:nc] + both[:, nc : 2 * nc]

    def own_sum(left, right):
        return jnp.sum(
            left[0 : 2 * lf, :] * right[0 : 2 * lf, :], axis=0, keepdims=True
        )

    def rows_in(r):
        return modes if r == 1 else modes + 1 if r == ROUNDS - 1 else modes + 3

    def stride(r):
        return 1 if r == ROUNDS - 1 else halves

    def spread_terms(r, rows):
        mine = terms.at[r, me_h, side, me_y, pl.ds(0, rows)]
        for tx in range(nx // stride(r)):
            for ty in range(ny):
                if tx or ty:
                    remote(
                        mine, mine, t_send.at[r - 1], t_recv.at[r - 1],
                        (lax.rem(me_x + stride(r) * tx, nx), lax.rem(me_y + ty, ny)),
                    ).start()

    def all_terms(r, rows):
        others = nx * ny // stride(r) - 1
        every = terms.at[r].reshape(nx * ny, 16, nc).at[pl.ds(0, others), pl.ds(0, rows)]
        return remote(
            every, every, t_send.at[r - 1], t_recv.at[r - 1], (me_x, lax.rem(me_y + 1, ny))
        )

    def pair_terms(r, rows):
        mine = terms.at[r, :, side, :, pl.ds(0, rows)]
        return remote(
            mine, mine, x_send.at[r - 1], x_recv.at[r - 1], (me_x + 1 - 2 * side, me_y)
        )

    def terms_arrived(r, rows):
        all_terms(r, rows).wait_recv()
        if stride(r) == 2:
            pair_terms(r, rows).start()
        if r < ROUNDS - 1:
            for f in (SOUTH, NORTH):
                face_arrived(r, f)
                inbox[r - 1, f] = applied(r, f)
        if stride(r) == 2:
            pair_terms(r, rows).wait_recv()

    def totals(r):
        return jnp.sum(terms[r, :, :, :, 0:16, :].reshape(nx * ny, 16, nc), axis=0)

    solve(0)
    gather_alpha()
    for f in range(2):
        mult_ref[face(f), :] = mode_image(f)

    l_copy.wait()
    for f in range(2):
        @pl.when(exists[2 + f])
        def _():
            loads_copy(f).wait_recv()
    for f in range(4):
        values = loads4[face(f), :]
        if f >= 2:
            high, mid, low = split3(values)
            both = dot32(swap[f], beside(high, mid))
            values = both[:, 0:nc] + (both[:, nc : 2 * nc] + dot32(swap[f], low))
        loads4[face(f), :] = values * free4[face(f), :]

    lanes = lax.broadcasted_iota(jnp.int32, (h, nc), 1)
    for f in (EAST, WEST, SOUTH, NORTH):
        @pl.when(exists[f])
        def _():
            g = OPPOSITE[f]
            remote(
                fold_out.at[g], fold_in.at[f], fold_send.at[g], fold_recv.at[f], place[f]
            ).wait_recv()

        came = fold_in[f]
        parts = []
        for b in range(PIECES):
            moved = came if b == 0 else pltpu.roll(came, nc - b * lane_step, 1)
            parts.append(jnp.where(lanes < lane_step, moved, 0.0))
        far = exchanged(f, rows_of(*parts))
        values = (fp_f[face(f), :] + pltpu.roll(far, lane_step, 1)) * free4[face(f), :]
        high, low = split(values)
        images[f, pl.ds(0, lf), :] = (
            high.astype(F32) + pltpu.roll(low.astype(F32), half, 1)
        ).astype(BF16)

    def put_field(f, values):
        high, low = split(values)
        vsplit[face(f), 0:nc] = high
        vsplit[face(f), nc : 2 * nc] = low

    for f in range(4):
        v = dual_mode_image(f) - loads4[face(f), :]
        put_field(f, v)
        if f < 2:
            p_f[face(f), :] = v

    coarse_terms(1)
    spread_terms(1, rows_in(1))
    apply_start(1)
    terms_arrived(1, rows_in(1))
    solve(1)
    gather_alpha()

    for f in range(4):
        fp_f[face(f), :] = dual_mode_image(f)
    for f in range(2):
        p = p_f[face(f), :] - mode_image(f)
        p_f[face(f), :] = p
        d_f[face(f), :] = p
    for f in (SOUTH, NORTH, EAST, WEST):
        q = finished(1, f) - fp_f[face(f), :]
        q_f[face(f), :] = q
        fp_f[face(f), :] = q
        put_field(f, q)

    norm = None
    for step in range(ITERS):
        r = step + 2
        last = step + 1 == ITERS
        rows = rows_in(r)
        coarse_terms(r)
        terms[r, me_h, side, me_y, modes : modes + 1, :] = own_sum(d_f, q_f)
        if not last:
            terms[r, me_h, side, me_y, modes + 1 : modes + 2, :] = own_sum(
                p_f, p_f if step == 0 else q_f
            )
            terms[r, me_h, side, me_y, modes + 2 : modes + 3, :] = own_sum(q_f, q_f)
        spread_terms(r, rows)
        if not last:
            apply_start(r)
        terms_arrived(r, rows)
        inner = solve(r)
        gather_alpha()
        total = totals(r)
        curvature = total[6:7, :]
        if step == 0:
            norm = total[7:8, :]
            cross = curvature
        else:
            cross = total[7:8, :]
        size = norm / curvature
        if last:
            mult_ref[...] = mult_ref[...] + size * d_f[...]
            for f in range(2):
                proj_ref[face(f), :] = p_f[face(f), :] + size * (q_f[face(f), :] - mode_image(f))
            break
        norm_next = norm + 2.0 * size * cross + size * size * (total[8:9, :] - inner)
        ratio = norm_next / norm
        for f in range(4):
            fp_f[face(f), :] = fp_f[face(f), :] - size * dual_mode_image(f)
        for f in range(2):
            d = d_f[face(f), :]
            p = p_f[face(f), :] + size * (q_f[face(f), :] - mode_image(f))
            mult_ref[face(f), :] = mult_ref[face(f), :] + size * d
            p_f[face(f), :] = p
            d_f[face(f), :] = p + ratio * d
        for f in (SOUTH, NORTH, EAST, WEST):
            fp = fp_f[face(f), :] + size * finished(r, f)
            fp_f[face(f), :] = fp
            q = fp + ratio * q_f[face(f), :]
            q_f[face(f), :] = q
            put_field(f, q)
        norm = norm_next

    for r in range(1, ROUNDS):
        rows = rows_in(r)
        all_terms(r, rows).wait_send()
        if stride(r) == 2:
            pair_terms(r, rows).wait_send()
    for stage in coarse_stages:
        column_all(stage).wait_send()
        row_all(stage).wait_send()
    for f in range(2):
        @pl.when(exists[f])
        def _():
            to_owned(f).wait_send()
            loads_copy(f).wait_send()

        @pl.when(exists[2 + f])
        def _():
            to_owner(f).wait_send()
    for f in range(4):
        @pl.when(exists[f])
        def _():
            fold_copy(f).wait_send()
            remote(
                outbox.at[:, f], inbox.at[:, f], face_send.at[f], face_recv.at[0, f], place[f]
            ).wait_send()


def solution(mesh):
    nx, ny = mesh.shape["gx"], mesh.shape["gy"]

    def local(dual_ops, loads, coarse_rhs, coarse_modes, free_mask, face_match, coarse_rows):
        lm = dual_ops.shape[-1]
        lf, nc = loads.shape[-2:]
        wide = nx * ny * 8
        halves = 2 if nx % 2 == 0 else 1
        vmem = pl.BlockSpec(memory_space=pltpu.VMEM)
        hbm = pl.BlockSpec(memory_space=pl.ANY)
        dma = pltpu.SemaphoreType.DMA
        out = jax.ShapeDtypeStruct((2 * lf, nc), F32)
        field = pltpu.VMEM((lm, nc), F32)
        own = pltpu.VMEM((2 * lf, nc), F32)
        mult, proj = pl.pallas_call(
            functools.partial(kernel, nx, ny),
            out_shape=(pltpu.VMEM((2 * lf, nc), F32),) * 2,
            in_specs=[hbm, hbm] + [vmem] * 5,
            out_specs=(vmem, vmem),
            scratch_shapes=[
                pltpu.VMEM((lm, lm), F32),
                pltpu.VMEM((lm, lm), BF16),
                pltpu.VMEM((lm, lm), BF16),
                field,
                pltpu.VMEM((2, 24, lf), F32),
                pltpu.VMEM((2, 24, lf), F32),
                pltpu.VMEM((2, 8, lf), F32),
                pltpu.VMEM((2, 8, lf), F32),
                pltpu.VMEM((nx, ny, 8, wide), F32),
                pltpu.VMEM((wide, 4 * wide), BF16),
                pltpu.VMEM((ROUNDS, nx // halves, halves, ny, 16, nc), F32),
                pltpu.VMEM((nx * ny, 8, nc), F32),
                pltpu.VMEM((4, nc // 2, nc), F32),
                pltpu.VMEM((16, lm), F32),
                pltpu.VMEM((16, lm), BF16),
                pltpu.VMEM((4, 2 * lf, nc), BF16),
                field,
                pltpu.VMEM((nc, lf), F32),
                pltpu.VMEM((4, lf, lf), BF16),
                pltpu.VMEM((lm, 2 * nc), BF16),
                pltpu.VMEM((4, lf // PIECES, nc), F32),
                pltpu.VMEM((4, lf // PIECES, nc), F32),
                pltpu.VMEM((APPLIES - 1, 4, lf, nc), F32),
                pltpu.VMEM((APPLIES - 1, 4, lf, nc), F32),
                own, own, field, field,
                dma((2 * PIECES,)),
                dma,
                dma((4,)),
                dma((APPLIES - 1, 4)),
                dma((4,)), dma((4,)),
                dma((2,)), dma((2,)), dma((2,)), dma((2,)), dma((2,)), dma((2,)),
                dma, dma, dma, dma, dma, dma, dma, dma,
                dma((ROUNDS - 1,)), dma((ROUNDS - 1,)), dma((ROUNDS - 1,)), dma((ROUNDS - 1,)),
            ],
            compiler_params=pltpu.CompilerParams(
                collective_id=0, has_side_effects=True, vmem_limit_bytes=60 * 1024 * 1024
            ),
        )(
            dual_ops.reshape(lm, lm),
            loads.reshape(2 * lf, nc),
            coarse_rhs.reshape(coarse_rhs.shape[2], 1, nc),
            jnp.swapaxes(coarse_modes.reshape(coarse_modes.shape[2:]), 1, 2),
            free_mask.reshape(free_mask.shape[2:]),
            face_match.reshape(face_match.shape[2:]),
            coarse_rows.reshape(-1, 1, coarse_rows.shape[-1]),
        )
        return (mult.reshape(1, 1, 2, lf, nc), proj.reshape(1, 1, 2, lf, nc))

    in_specs = (
        P("gx", "gy", None, None),
        P("gx", "gy", None, None, None),
        P("gx", "gy", None, None),
        P("gx", "gy", None, None, None, None),
        P("gx", "gy", None, None),
        P("gx", "gy", None, None),
        P("gx", "gy", None, None, None),
    )
    out_specs = (P("gx", "gy", None, None, None), P("gx", "gy", None, None, None))
    return jax.shard_map(local, mesh=mesh, in_specs=in_specs, out_specs=out_specs, check_vma=False)
```
